32 devices in a mesh: gx: 4 (over z), gy: 4 (over y, x), gz: 2 (over core).
Axes of the slice: x: 2, y: 2, z: 4, core: 2. Of those that a mesh axis runs over, the one named last changes fastest.
Arguments:
- positions: float32 [3, 4096], P(None, ('gx', 'gy', 'gz')), may hold values from 0 to 4.5
- species: int32 [4096], P(('gx', 'gy', 'gz')), may hold values from 0 to 88
- cell_map: int32 [32, 128], P(('gx', 'gy', 'gz')), may hold values from 0 to 127, each once within a row
- neighbours: int32 [8, 4096], P(None, ('gx', 'gy', 'gz')), may hold values from 0 to 511
- struct_ids: int32 [4096], P(('gx', 'gy', 'gz')), may hold values from 0 to 15, as said below
- embed: float32 [89, 128], replicated, may hold values from -6 to 6
- w_up: float32 [2, 128, 128], replicated, may hold values from -0.5 to 0.5
- w_rad_in: float32 [2, 8, 64], replicated, may hold values from -2 to 2
- w_rad_out: float32 [2, 64, 256], replicated, may hold values from -0.75 to 0.75
- w_mix: float32 [2, 3, 128, 128], replicated, may hold values from -0.5 to 0.5
- read_first: float32 [128], replicated, may hold values from -0.5 to 0.5
- read_hidden: float32 [128, 16], replicated, may hold values from -0.5 to 0.5
- read_last: float32 [16], replicated, may hold values from -1.5 to 1.5
Outputs:
- energies: float32 [16], replicated
- virials: float32 [9, 16], replicated
- forces: float32 [3, 4096], P(None, ('gx', 'gy', 'gz'))
The draws below stay inside these ranges and needn't reach their ends.
Inputs may be any that keep to these rules, and one draw needn't show every extreme that they name: `cell_map`: each row is a permutation. `neighbours`: entries index the extended rows of the atom's own device. `struct_ids`: atoms of the devices with gx index a have ids from a * 4 to (a + 1) * 4 - 1.
All inputs are finite; a program needn't handle non-finite values.
Results may differ from the reference program's by a relative error of at most 0.0003.
Values sent between devices are 32-bit elements; how exact they have to be, the bound alone decides.
A program may use at most 64 MiB of HBM per device.

```python
import math
import jax
import jax.numpy as jnp
from jax import lax

C = 128
NB = 8
H = 64
RH = 16
SPECIES = 89
NEIGH = 8
A_DEV = 128
SLAB_STRUCTS = 4
FACE_ATOMS = 64
EXTENDED = 512
ATOMS = 4096
SLAB_ATOMS = 1024
STRUCTS = 16
N_GX = 4
N_GY = 4
N_GZ = 2
DEVICES = 32


def draw_struct_ids(key, part):
    atom_index = jnp.arange(ATOMS, dtype=jnp.int32)
    slab_index = atom_index // SLAB_ATOMS
    within = jax.random.randint(key, (ATOMS,), 0, SLAB_STRUCTS, dtype=jnp.int32)
    return slab_index * SLAB_STRUCTS + within


def touch_ends(values, own_key, low, top_value):
    shape = values.shape
    spot = [jax.random.randint(jax.random.fold_in(own_key, axis), (), 0, shape[axis]) for axis in range(len(shape))]
    values = values.at[tuple(spot)].set(low)
    longest = shape.index(max(shape))
    spot[longest] = (spot[longest] + 1) % shape[longest]
    return values.at[tuple(spot)].set(top_value)


def block_levels(rng, extent, shards, least, high):
    def one(position, blocks):
        heights = jax.random.uniform(jax.random.fold_in(jax.random.fold_in(rng, 6), position), (blocks,), jnp.float32, least / len(shards), high / len(shards))
        return jnp.repeat(jnp.exp(heights), extent[position] // blocks).reshape((-1,) + (1,) * (len(extent) - position - 1))

    level = one(*shards[0])
    for cut in shards[1:]:
        level = level * one(*cut)
    return level


def gaussian(own_key, shape, width, limit, kind=jnp.bfloat16):
    values = jax.random.normal(own_key, shape, jnp.float32) * width
    return jnp.minimum(jnp.maximum(values, -limit), limit).astype(kind)


def setup_inputs(seed: int = 0) -> dict:
    splits = jax.random.split(jax.random.key(seed), 14)
    positions = jnp.clip(4.5 * jax.random.uniform(splits[0], (3, ATOMS), jnp.float32) ** block_levels(splits[0], (3, ATOMS), ((1, 32),), -0.2, 0.2), 0.0, 4.5)
    species = touch_ends(jax.random.randint(splits[1], (ATOMS,), 0, SPECIES), jax.random.fold_in(splits[1], 1), 0, SPECIES - 1).astype(jnp.int32)
    cell_map = jax.vmap(lambda own: jax.random.permutation(own, A_DEV))(jax.random.split(splits[2], DEVICES)).reshape((DEVICES, A_DEV)).astype(jnp.int32)
    neighbours = touch_ends(jax.random.randint(splits[3], (NEIGH, ATOMS), 0, EXTENDED), jax.random.fold_in(splits[3], 1), 0, EXTENDED - 1).astype(jnp.int32)
    struct_ids = draw_struct_ids(jax.random.fold_in(splits[13], 71), 0)
    embed = gaussian(splits[5], (SPECIES, C), 1.0, 6.0, jnp.float32)
    w_up = gaussian(splits[6], (2, C, C), C ** -0.5, 0.5, jnp.float32)
    w_rad_in = gaussian(splits[7], (2, NB, H), NB ** -0.5, 2.0, jnp.float32)
    w_rad_out = gaussian(splits[8], (2, H, 2 * C), H ** -0.5, 0.75, jnp.float32)
    w_mix = gaussian(splits[9], (2, 3, C, C), C ** -0.5, 0.5, jnp.float32)
    read_first = gaussian(splits[10], (C,), C ** -0.5, 0.5, jnp.float32)
    read_hidden = gaussian(splits[11], (C, RH), C ** -0.5, 0.5, jnp.float32)
    read_last = gaussian(splits[12], (RH,), RH ** -0.5, 1.5, jnp.float32)
    return dict(positions=positions, species=species, cell_map=cell_map, neighbours=neighbours, struct_ids=struct_ids, embed=embed, w_up=w_up, w_rad_in=w_rad_in, w_rad_out=w_rad_out, w_mix=w_mix, read_first=read_first, read_hidden=read_hidden, read_last=read_last)


precise = lax.Precision.HIGHEST
cutoff = 6.0
box_side = 4.5
soften = 0.25

def matmul(left, right):
    return jnp.dot(left, right, precision=precise, preferred_element_type=jnp.float32)

def edge_terms(edge_vec, bessels):
    radius = jnp.sqrt(lax.optimization_barrier(jnp.sum(edge_vec * edge_vec, axis=0)) + soften)
    envelope = jnp.square(jax.nn.relu(1.0 - radius * radius / (cutoff * cutoff)))
    harmonic = jnp.arange(1, bessels + 1).astype(jnp.float32)
    angles = harmonic[:, None, None] * (jnp.pi / cutoff) * radius[None]
    bessel = math.sqrt(2.0 / cutoff) * jnp.sin(angles) / radius[None] * envelope[None]
    return (bessel, edge_vec / radius[None])

def interact(edge_vec, feats_ext, nbr_slots, w_up, w_rad_in, w_rad_out, w_mix):
    bessel, direction = edge_terms(edge_vec, w_rad_in.shape[0])
    hidden = jax.nn.silu(jnp.einsum('nka,nh->kah', bessel, w_rad_in, precision=precise))
    radial = jnp.einsum('kah,hc->kac', hidden, w_rad_out, precision=precise)
    lifted = matmul(feats_ext, w_up)
    picked = lifted[nbr_slots]
    channels = lifted.shape[1]
    scaling = 1.0 / math.sqrt(nbr_slots.shape[0])
    scalar = lax.optimization_barrier(jnp.sum(radial[:, :, :channels] * picked, axis=0)) * scaling
    vector = jnp.einsum('mka,kac->mac', direction, radial[:, :, channels:] * picked, precision=precise) * scaling
    squares = lax.optimization_barrier(jnp.sum(vector * vector, axis=0))
    return matmul(scalar, w_mix[0]) + matmul(squares, w_mix[1]) + matmul(scalar * scalar, w_mix[2])

def atom_energy(layer_out, second, read_first, read_hidden, read_last):
    hidden = jax.nn.silu(matmul(second, read_hidden))
    return matmul(layer_out, read_first) + matmul(hidden, read_last)

def to_cells(grid_rows, cell_order):
    picked = jnp.take_along_axis(grid_rows, cell_order[..., None], axis=3)
    shape = grid_rows.shape
    return picked.reshape(shape[:3] + (2, 2, 2, shape[3] // 8, shape[4]))

def face_rows(cell_data):
    pieces = (jnp.roll(cell_data, 1, axis=0)[:, :, :, 1], jnp.roll(cell_data, -1, axis=0)[:, :, :, 0], jnp.roll(cell_data, 1, axis=1)[:, :, :, :, 1], jnp.roll(cell_data, -1, axis=1)[:, :, :, :, 0], jnp.roll(cell_data, 1, axis=2)[:, :, :, :, :, 1], jnp.roll(cell_data, -1, axis=2)[:, :, :, :, :, 0])
    return jnp.concatenate([piece.reshape(piece.shape[:3] + (-1, piece.shape[-1])) for piece in pieces], axis=3)

def scatter_rows(cell_order, values):
    return jnp.zeros_like(values).at[cell_order].add(values)

def return_rows(ghosts, cell_order):
    shape = ghosts.shape
    per_face = shape[3] // 6
    per_cell = per_face // 4
    channels = shape[4]
    pieces = ghosts.reshape(shape[:3] + (6, 2, 2, per_cell, channels))
    cell_sums = jnp.zeros(shape[:3] + (2, 2, 2, per_cell, channels), jnp.float32)
    cell_sums = cell_sums.at[:, :, :, 1].add(jnp.roll(pieces[:, :, :, 0], -1, axis=0))
    cell_sums = cell_sums.at[:, :, :, 0].add(jnp.roll(pieces[:, :, :, 1], 1, axis=0))
    cell_sums = cell_sums.at[:, :, :, :, 1].add(jnp.roll(pieces[:, :, :, 2], -1, axis=1))
    cell_sums = cell_sums.at[:, :, :, :, 0].add(jnp.roll(pieces[:, :, :, 3], 1, axis=1))
    cell_sums = cell_sums.at[:, :, :, :, :, 1].add(jnp.roll(pieces[:, :, :, 4], -1, axis=2))
    cell_sums = cell_sums.at[:, :, :, :, :, 0].add(jnp.roll(pieces[:, :, :, 5], 1, axis=2))
    devices = shape[0] * shape[1] * shape[2]
    flat_sums = cell_sums.reshape(devices, 8 * per_cell, channels)
    return jax.vmap(scatter_rows)(cell_order.reshape(devices, -1), flat_sums)

def pick_rows(table_rows, slots):
    return table_rows[slots]

def scatter_edges(slots, grads):
    flat_grad = grads.transpose(1, 2, 0).reshape(-1, 3)
    return jnp.zeros((EXTENDED, 3), jnp.float32).at[slots.reshape(-1)].add(flat_grad)

def reference(positions, species, cell_map, neighbours, struct_ids, embed, w_up, w_rad_in, w_rad_out, w_mix, read_first, read_hidden, read_last):
    dev_grid = (N_GX, N_GY, N_GZ)
    devices = N_GX * N_GY * N_GZ
    atom_count = A_DEV
    channels = embed.shape[1]
    cell_order = cell_map.reshape(dev_grid + (atom_count,))
    pos_rows = positions.reshape((3,) + dev_grid + (atom_count,)).transpose(1, 2, 3, 4, 0)
    shifts = jnp.array([[-box_side, 0.0, 0.0], [box_side, 0.0, 0.0], [0.0, -box_side, 0.0], [0.0, box_side, 0.0], [0.0, 0.0, -box_side], [0.0, 0.0, box_side]], jnp.float32)
    ghost_pos = face_rows(to_cells(pos_rows, cell_order)) + jnp.repeat(shifts, FACE_ATOMS, axis=0)
    ext_pos = jnp.concatenate([pos_rows, ghost_pos], axis=3).reshape(devices, EXTENDED, 3)
    nbr_slots = neighbours.reshape(NEIGH, devices, atom_count).transpose(1, 0, 2)
    far_rows = jax.vmap(pick_rows)(ext_pos, nbr_slots)
    edge_vec = (far_rows - pos_rows.reshape(devices, 1, atom_count, 3)).transpose(0, 3, 1, 2)
    one_hot = (species[:, None] == jnp.arange(embed.shape[0])[None]).astype(jnp.float32)
    initial = matmul(one_hot, embed).reshape(dev_grid + (atom_count, channels))
    initial_ext = jnp.concatenate([initial, face_rows(to_cells(initial, cell_order))], axis=3).reshape(devices, EXTENDED, channels)
    initial_flat = initial.reshape(devices, atom_count, channels)

    def layer_zero(packed):
        return interact(packed[0], packed[1], packed[2], w_up[0], w_rad_in[0], w_rad_out[0], w_mix[0])

    def layer_one(packed):
        return interact(packed[0], packed[1], packed[2], w_up[1], w_rad_in[1], w_rad_out[1], w_mix[1])
    step_zero = jax.checkpoint(layer_zero)
    step_one = jax.checkpoint(layer_one)

    def energies_of(edges):
        layer_out = initial_flat + lax.map(step_zero, (edges, initial_ext, nbr_slots))
        out_grid = layer_out.reshape(dev_grid + (atom_count, channels))
        out_ext = jnp.concatenate([out_grid, face_rows(to_cells(out_grid, cell_order))], axis=3).reshape(devices, EXTENDED, channels)
        second = layer_out + lax.map(step_one, (edges, out_ext, nbr_slots))
        return atom_energy(layer_out.reshape(-1, channels), second.reshape(-1, channels), read_first, read_hidden, read_last)
    atom_e, pullback = jax.vjp(energies_of, edge_vec)
    edge_grad, = pullback(jnp.ones_like(atom_e))
    scattered = jax.vmap(scatter_edges)(nbr_slots, edge_grad)
    own_grad = scattered[:, :atom_count] - lax.optimization_barrier(jnp.sum(edge_grad, axis=2)).transpose(0, 2, 1)
    returned = return_rows(scattered[:, atom_count:].reshape(dev_grid + (6 * FACE_ATOMS, 3)), cell_order)
    forces = -(own_grad + returned)
    forces = forces.transpose(2, 0, 1).reshape(3, ATOMS)
    outer_sums = -jnp.einsum('dakx,dbkx->abdx', edge_vec, edge_grad, precision=precise).reshape(9, ATOMS)
    member = (struct_ids[None] == jnp.arange(STRUCTS)[:, None]).astype(jnp.float32)
    energies = matmul(member, atom_e)
    virials = matmul(outer_sums, member.T)
    return (energies, virials, forces)
```

```python
import functools
import math

import jax
import jax.numpy as jnp
from jax import lax
from jax.experimental import pallas as pl
from jax.experimental.pallas import tpu as pltpu
from jax.sharding import PartitionSpec as P

SLAB_STRUCTS = 4
AXES = ("gx", "gy", "gz")
MESH = pl.DeviceIdType.MESH
cutoff = 6.0
box_side = 4.5
soften = 0.25
f32 = jnp.float32
bf16 = jnp.bfloat16


def split2(x):
    high = x.astype(bf16)
    return high, (x - high.astype(f32)).astype(bf16)


def parts3(x):
    high = x.astype(bf16).astype(f32)
    rest = x - high
    mid = rest.astype(bf16).astype(f32)
    return jnp.concatenate([high, mid, rest - mid], axis=0)


def dot(left, right, dims):
    return lax.dot_general(
        left, right, (((dims[0],), (dims[1],)), ((), ())), preferred_element_type=f32
    )


def dot3(left, right, dims):
    lh, ll = split2(left)
    rh, rl = split2(right)
    return dot(lh, rh, dims) + (dot(lh, rl, dims) + dot(ll, rh, dims))


def dot3_tall(left, right):
    lh = left.astype(bf16).astype(f32)
    rh = right.astype(bf16).astype(f32)
    lefts = jnp.concatenate([lh, lh, left - lh], axis=0).astype(bf16)
    rights = jnp.concatenate([rh, right - rh, rh], axis=0).astype(bf16)
    return dot(lefts, rights, (0, 0))


def pick(table, chosen):
    width = table.shape[0]
    both = dot(jnp.concatenate(split2(table), axis=0), chosen, (1, 0))
    return both[:width] + both[width:]


def to_col(row):
    n = row.shape[1]
    same = lax.broadcasted_iota(jnp.int32, (n, n), 0) == lax.broadcasted_iota(jnp.int32, (n, n), 1)
    return jnp.sum(jnp.where(same, jnp.broadcast_to(row, (n, n)), 0.0), axis=1, keepdims=True)


def sigmoid(x):
    return 1.0 / (1.0 + jnp.exp(-x))


def sin_cos_pi(turns):
    near = jnp.floor(turns + 0.5)
    x = (turns - near) * math.pi
    sign = 1.0 - 2.0 * (near - 2.0 * jnp.floor(near * 0.5))
    x2 = x * x
    s = jnp.full_like(x, 1.0 / math.factorial(13))
    for p in (11, 9, 7, 5, 3, 1):
        s = s * x2 + (-1.0) ** ((p - 1) // 2) / math.factorial(p)
    c = jnp.full_like(x, 1.0 / math.factorial(12))
    for p in (10, 8, 6, 4, 2, 0):
        c = c * x2 + (-1.0) ** (p // 2) / math.factorial(p)
    return s * x * sign, c * sign


def kernel(
    counts,
    pos, spe, cmap, nbr, sid, embed, w_up, w_ri, w_ro, w_mix, rfirst, rhid, rlast,
    en_out, vir_out, f_out,
    stage, emb, oh, soh, dirs, pre, rad, picked, grads, d_rad, d_pick, ddir, feats,
    sendp, sends, recvp, reccs, lsend, tables, back, backs, fsend, frecv, red, redstage,
    slab_buf, gx_send, gx_buf,
    p_s, p_r, s_s, s_r, l_s, l_r, b_s, b_r, f_s, f_r, a_s, a_r, g_s, g_r,
):
    nx, ny, nz = counts
    size = dict(zip(AXES, counts))
    me = {axis: lax.axis_index(axis) for axis in AXES}
    atoms = pos.shape[1]
    neigh = nbr.shape[0]
    edges = neigh * atoms
    chans = embed.shape[1]
    per_cell = atoms // 8
    scaling = 1.0 / math.sqrt(neigh)

    def at(shift):
        return {
            axis: lax.rem(me[axis] + (step % size[axis]), size[axis])
            for axis, step in zip(AXES, shift)
            if step % size[axis]
        }

    slab_shifts = [(0, j, k) for j in range(ny) for k in range(nz) if (j, k) != (0, 0)]
    gx_shifts = [(i, 0, 0) for i in range(1, nx)]
    peers = slab_shifts + gx_shifts
    barrier = pltpu.get_barrier_semaphore()
    for shift in peers:
        pl.semaphore_signal(barrier, inc=1, device_id=at(shift), device_id_type=MESH)

    def face_shift(axis, step):
        return tuple(step if a == axis else 0 for a in range(3))

    def remote(src, dst, send, recv, shift):
        return pltpu.make_async_remote_copy(
            src_ref=src, dst_ref=dst, send_sem=send, recv_sem=recv,
            device_id=at(shift), device_id_type=MESH,
        )

    stage[...] = jnp.zeros_like(stage)
    stage[0:neigh, :] = nbr[...].astype(f32)
    base = stage.shape[0] - 8
    stage[base : base + 3, :] = pos[...]
    stage[base + 3 : base + 4, :] = spe[...].astype(f32)
    stage[base + 4 : base + 5, :] = sid[...].astype(f32)
    iota0 = lax.broadcasted_iota(jnp.int32, (atoms, atoms), 0)
    iota1 = lax.broadcasted_iota(jnp.int32, (atoms, atoms), 1)
    cm_row = cmap[...]
    order_t = jnp.where(iota0 == cm_row, 1.0, 0.0).astype(bf16)
    height = stage.shape[0]
    moved = dot(parts3(stage[...]).astype(bf16), order_t, (1, 0))
    moved = moved[:height] + moved[height : 2 * height] + moved[2 * height :]
    nbr_c = moved[0:neigh].astype(jnp.int32)
    tail = moved[base : base + 8]
    row8 = lax.broadcasted_iota(jnp.int32, (8, atoms), 0)
    pos_c = jnp.where(row8 < 3, tail, 0.0)
    spe_c = tail[3:4].astype(jnp.int32)
    sid_c = tail[4:5].astype(jnp.int32)
    sendp[...] = pos_c
    sends[...] = jnp.broadcast_to(spe_c, (8, atoms))

    pl.semaphore_wait(barrier, len(peers))
    copies = []
    for axis in range(3):
        for face, step in ((2 * axis, 1), (2 * axis + 1, -1)):
            copies.append(remote(sendp, recvp.at[face], p_s.at[face], p_r.at[face], face_shift(axis, step)))
            copies.append(remote(sends, reccs.at[face], s_s.at[face], s_r.at[face], face_shift(axis, step)))
    for copy in copies:
        copy.start()

    cm_col = to_col(cm_row.astype(f32)).astype(jnp.int32)
    own_slot = jnp.broadcast_to(cm_col, (atoms, atoms))
    half = atoms // 2
    bits = [(iota0 // (per_cell * w)) % 2 for w in (4, 2, 1)]
    inner = iota0 % per_cell
    ids = [own_slot]
    for axis in range(3):
        others = [bits[a] for a in range(3) if a != axis]
        ids.append(
            (axis + 1) * atoms + (1 - bits[axis]) * half
            + others[0] * (2 * per_cell) + others[1] * per_cell + inner
        )
    for t in range(4):
        for k in range(neigh):
            oh[t * atoms : (t + 1) * atoms, k * atoms : (k + 1) * atoms] = jnp.where(
                ids[t] == nbr_c[k : k + 1], 1.0, 0.0
            ).astype(bf16)
    elements = embed.shape[0]
    emb[...] = jnp.zeros_like(emb)
    emb[0:elements, :] = embed[...]
    table = emb[...]
    lifted_zero = dot3(table, w_up[0], (1, 0)).T
    el_iota = lax.broadcasted_iota(jnp.int32, (table.shape[0], atoms), 0)
    own_el = jnp.where(el_iota == spe_c, 1.0, 0.0).astype(bf16)
    initial = pick(table.T, own_el)
    first_col = to_col(rfirst[...])
    last_col = to_col(rlast[...])

    for copy in copies:
        copy.wait()

    lane_bits = [(lax.broadcasted_iota(jnp.int32, (8, atoms), 1) // (per_cell * w)) % 2 for w in (4, 2, 1)]
    pieces = [jnp.where(row8 == 3, jnp.broadcast_to(spe_c, (8, atoms)).astype(f32), pos_c)]
    for axis in range(3):
        low = lane_bits[axis] == 1
        where_pos = jnp.where(low, recvp[2 * axis], recvp[2 * axis + 1])
        shifted = where_pos + jnp.where(low, -box_side, box_side)
        where_pos = jnp.where(row8 == axis, shifted, where_pos)
        where_el = jnp.where(low, reccs[2 * axis], reccs[2 * axis + 1]).astype(f32)
        pieces.append(jnp.where(row8 == 3, where_el, where_pos))
    ext = jnp.concatenate(pieces, axis=1)
    ext3 = jnp.concatenate([parts3(ext), jnp.zeros_like(ext)], axis=0).astype(bf16)
    far = dot(ext3, oh[...], (1, 0))
    far = far[0:8] + far[8:16] + far[16:24]
    ev = far - jnp.concatenate([pos_c] * neigh, axis=1)
    far_el = far[3:4].astype(jnp.int32)
    for k in range(neigh):
        cols = slice(k * atoms, (k + 1) * atoms)
        soh[:, cols] = jnp.where(el_iota == far_el[:, cols], 1.0, 0.0).astype(bf16)
    r2 = ev[0:1] * ev[0:1] + ev[1:2] * ev[1:2] + ev[2:3] * ev[2:3]
    radius = jnp.sqrt(r2 + soften)
    inv = 1.0 / radius
    room = jnp.maximum(0.0, 1.0 - radius * radius / (cutoff * cutoff))
    env = room * room
    d_env = room * radius * (-4.0 / (cutoff * cutoff))
    bessels = w_ri.shape[1]
    harm = (lax.broadcasted_iota(jnp.int32, (bessels, edges), 0) + 1).astype(f32)
    sn, cs = sin_cos_pi(harm * (radius * (1.0 / cutoff)))
    amp = math.sqrt(2.0 / cutoff) * inv
    bessel = sn * (amp * env)
    d_bessel = amp * (env * (harm * (math.pi / cutoff) * cs - sn * inv) + sn * d_env)
    dirs[...] = ev * inv

    chunk = 32

    def radial(layer):
        x = dot3_tall(w_ri[layer], bessel)
        pre[layer] = x
        rad[layer] = dot3_tall(w_ro[layer], x * sigmoid(x))

    def forward(layer):
        for c in range(0, chans, chunk):
            s = v0 = v1 = v2 = None
            for k in range(neigh):
                cols = pl.ds(k * atoms, atoms)
                p = picked[layer, pl.ds(c, chunk), cols]
                a = rad[layer, pl.ds(c, chunk), cols] * p
                b = rad[layer, pl.ds(chans + c, chunk), cols] * p
                d = [dirs[pl.ds(m, 1), cols] for m in range(3)]
                if k == 0:
                    s, v0, v1, v2 = a, d[0] * b, d[1] * b, d[2] * b
                else:
                    s, v0, v1, v2 = s + a, v0 + d[0] * b, v1 + d[1] * b, v2 + d[2] * b
            s = s * scaling
            vs = [v * scaling for v in (v0, v1, v2)]
            rows = pl.ds(c, chunk)
            for m in range(3):
                feats[layer, 3 + m, rows, :] = vs[m]
            feats[layer, 0, rows, :] = s
            feats[layer, 1, rows, :] = vs[0] * vs[0] + vs[1] * vs[1] + vs[2] * vs[2]
            feats[layer, 2, rows, :] = s * s
        stacked = feats[layer, 0:3].reshape(3 * chans, atoms)
        return dot3(w_mix[layer].reshape(3 * chans, chans), stacked, (0, 0))

    def backward(layer, d_mix, with_pick):
        d_st = dot3(w_mix[layer].reshape(3 * chans, chans), d_mix, (1, 0))
        d_s = d_st[0:chans] + 2.0 * feats[layer, 0] * d_st[2 * chans :]
        grads[0] = d_s * scaling
        twice = d_st[chans : 2 * chans] * (2.0 * scaling)
        for m in range(3):
            grads[1 + m] = feats[layer, 3 + m] * twice
        for k in range(neigh):
            cols = pl.ds(k * atoms, atoms)
            d = [dirs[pl.ds(m, 1), cols] for m in range(3)]
            acc = [jnp.zeros((8, atoms), f32)] * 3
            for c in range(0, chans, chunk):
                rows = pl.ds(c, chunk)
                g = [grads[m, rows, :] for m in range(4)]
                p = picked[layer, rows, cols]
                b = rad[layer, pl.ds(chans + c, chunk), cols]
                t = d[0] * g[1] + d[1] * g[2] + d[2] * g[3]
                d_rad[rows, cols] = g[0] * p
                d_rad[pl.ds(chans + c, chunk), cols] = t * p
                if with_pick:
                    d_pick[rows, cols] = g[0] * rad[layer, rows, cols] + t * b
                q = b * p
                acc = [
                    acc[m] + jnp.sum((g[1 + m] * q).reshape(chunk // 8, 8, atoms), axis=0)
                    for m in range(3)
                ]
            for m in range(3):
                ddir[layer, pl.ds(m, 1), cols] = jnp.sum(acc[m], axis=0, keepdims=True)

    def backward_radial(layer):
        d_hidden = dot3(w_ro[layer], d_rad[...], (1, 0))
        x = pre[layer]
        sig = sigmoid(x)
        return dot3(w_ri[layer], d_hidden * sig * (1.0 + x * (1.0 - sig)), (1, 0))

    ddir[...] = jnp.zeros_like(ddir)
    radial(0)
    picked[0] = pick(lifted_zero, soh[...])
    layer_out = initial + forward(0)
    lifted = dot3(layer_out, w_up[1], (0, 0))
    grid = (2, 2, 2, per_cell, chans)
    lsend[...] = lifted.reshape(grid)

    def part(ref, axis, side):
        return ref.at[(slice(None),) * axis + (side,)]

    copies = []
    for axis in range(3):
        for side, step in ((1, 1), (0, -1)):
            i = 2 * axis + side
            copies.append(
                remote(part(lsend, axis, side), part(tables.at[axis], axis, side), l_s.at[i], l_r.at[i], face_shift(axis, step))
            )
    for copy in copies:
        copy.start()
    radial(1)
    own_pick = pick(lifted.T, oh[0:atoms, :])
    for copy in copies:
        copy.wait()
    ghosts = jnp.concatenate([tables[a].reshape(atoms, chans).T for a in range(3)], axis=1)
    picked[1] = own_pick + pick(ghosts, oh[atoms:, :])
    second = layer_out + forward(1)
    x2 = dot3(rhid[...], second, (0, 0))
    sig2 = sigmoid(x2)
    energy = jnp.sum(first_col * layer_out, axis=0, keepdims=True) + jnp.sum(
        last_col * (x2 * sig2), axis=0, keepdims=True
    )
    d_second = dot3(rhid[...], last_col * (sig2 * (1.0 + x2 * (1.0 - sig2))), (1, 0))
    backward(1, d_second, True)
    d_ext = dot(oh[...], jnp.concatenate(split2(d_pick[...]), axis=0), (1, 1))
    d_ext = d_ext[:, :chans] + d_ext[:, chans:]
    for axis in range(3):
        back[axis] = d_ext[(axis + 1) * atoms : (axis + 2) * atoms].reshape(grid)
    copies = []
    for axis in range(3):
        for side, step in ((1, -1), (0, 1)):
            i = 2 * axis + side
            copies.append(
                remote(part(back.at[axis], axis, side), part(backs.at[axis], axis, side), b_s.at[i], b_r.at[i], face_shift(axis, step))
            )
    for copy in copies:
        copy.start()
    d_bes = backward_radial(1)
    for copy in copies:
        copy.wait()
    d_lifted = d_ext[0:atoms]
    for axis in range(3):
        d_lifted = d_lifted + backs[axis].reshape(atoms, chans)
    d_layer = d_second + first_col + dot3(w_up[1], d_lifted, (1, 1))
    backward(0, d_layer, False)
    d_bes = d_bes + backward_radial(0)
    d_dir = ddir[0] + ddir[1]
    along = d_dir * ev
    d_radius = jnp.sum(d_bes * d_bessel, axis=0, keepdims=True) - (
        along[0:1] + along[1:2] + along[2:3]
    ) * (inv * inv)
    edge_row = lax.broadcasted_iota(jnp.int32, (8, edges), 0)
    eg = jnp.where(edge_row < 3, d_dir * inv + ev * (d_radius * inv), 0.0)

    redstage[...] = jnp.zeros_like(redstage)

    def over_slots(x):
        total = x[:, 0:atoms]
        for k in range(1, neigh):
            total = total + x[:, k * atoms : (k + 1) * atoms]
        return total

    for r in range(3):
        redstage[3 * r : 3 * r + 3, :] = -over_slots(ev[r : r + 1] * eg)[0:3]
    redstage[9:10, :] = energy
    structs = SLAB_STRUCTS * nx
    member = jnp.where(
        lax.broadcasted_iota(jnp.int32, (structs, atoms), 0) == sid_c, 1.0, 0.0
    ).astype(bf16)
    shares = dot(parts3(redstage[...]).astype(bf16), member, (1, 1))
    shares = shares[0:16] + shares[16:32] + shares[32:48]
    red[...] = shares
    my_slot = me["gy"] * nz + me["gz"]
    sums = []
    for i, shift in enumerate(slab_shifts):
        sums.append(remote(red, slab_buf.at[my_slot], a_s.at[i], a_r.at[i], shift))
    for copy in sums:
        copy.start()

    eg3 = jnp.concatenate([parts3(eg), jnp.zeros_like(eg)], axis=0).astype(bf16)
    spread = dot(eg3, oh[...], (1, 1))
    spread = spread[0:8] + spread[8:16] + spread[16:24]
    for axis in range(3):
        fsend[axis] = spread[:, (axis + 1) * atoms : (axis + 2) * atoms]
    copies = []
    for axis in range(3):
        for face, step in ((2 * axis, -1), (2 * axis + 1, 1)):
            copies.append(remote(fsend.at[axis], frecv.at[face], f_s.at[face], f_r.at[face], face_shift(axis, step)))
    for copy in copies:
        copy.start()
    own = spread[:, 0:atoms] - over_slots(eg)
    slab_buf[my_slot] = red[...]
    for copy in sums:
        copy.wait()
    total = slab_buf[0]
    for i in range(1, ny * nz):
        total = total + slab_buf[i]
    gx_send[...] = total
    sums = []
    for i, shift in enumerate(gx_shifts):
        sums.append(remote(gx_send, gx_buf.at[i], g_s.at[i], g_r.at[i], shift))
    for copy in sums:
        copy.start()
    for copy in copies:
        copy.wait()
    for axis in range(3):
        own = own + jnp.where(lane_bits[axis] == 1, frecv[2 * axis], frecv[2 * axis + 1])
    order = jnp.where(own_slot == iota1, 1.0, 0.0).astype(bf16)
    own3 = jnp.concatenate([parts3(-own), jnp.zeros_like(own)], axis=0).astype(bf16)
    forces = dot(own3, order, (1, 0))
    f_out[...] = (forces[0:8] + forces[8:16] + forces[16:24])[0:3]
    for copy in sums:
        copy.wait()
    for i in range(len(gx_shifts)):
        total = total + gx_buf[i]
    vir_out[...] = total[0:9]
    en_out[...] = total[9:10]


def shards(counts, *args):
    (positions, species, cell_map, neighbours, struct_ids, embed, w_up, w_rad_in, w_rad_out,
     w_mix, read_first, read_hidden, read_last) = args
    nx, ny, nz = counts
    atoms = positions.shape[1]
    neigh = neighbours.shape[0]
    edges = neigh * atoms
    chans = embed.shape[1]
    hidden = w_rad_in.shape[2]
    per_cell = atoms // 8
    structs = SLAB_STRUCTS * nx
    el_rows = -(-embed.shape[0] // 128) * 128
    grid = (2, 2, 2, per_cell, chans)
    dma = pltpu.SemaphoreType.DMA
    vm = lambda *shape: pltpu.VMEM(shape, f32)
    vmem = pl.BlockSpec(memory_space=pltpu.VMEM)
    energies, virials, forces = pl.pallas_call(
        functools.partial(kernel, counts),
        out_shape=(
            jax.ShapeDtypeStruct((1, structs), f32),
            jax.ShapeDtypeStruct((9, structs), f32),
            jax.ShapeDtypeStruct((3, atoms), f32),
        ),
        in_specs=[vmem] * 13,
        out_specs=(vmem, vmem, vmem),
        scratch_shapes=[
            vm(-(-neigh // 8) * 8 + 8, atoms),
            vm(el_rows, chans),
            pltpu.VMEM((4 * atoms, edges), bf16),
            pltpu.VMEM((el_rows, edges), bf16),
            vm(8, edges),
            vm(2, hidden, edges),
            vm(2, 2 * chans, edges),
            vm(2, chans, edges),
            vm(4, chans, atoms),
            vm(2 * chans, edges),
            vm(chans, edges),
            vm(2, 8, edges),
            vm(2, 6, chans, atoms),
            vm(8, atoms),
            pltpu.VMEM((8, atoms), jnp.int32),
            vm(6, 8, atoms),
            pltpu.VMEM((6, 8, atoms), jnp.int32),
            vm(*grid),
            vm(3, *grid),
            vm(3, *grid),
            vm(3, *grid),
            vm(3, 8, atoms),
            vm(6, 8, atoms),
            vm(16, structs),
            vm(16, atoms),
            vm(ny * nz, 16, structs),
            vm(16, structs),
            vm(max(nx - 1, 1), 16, structs),
        ]
        + [dma((6,))] * 10
        + [dma((ny * nz - 1,))] * 2
        + [dma((max(nx - 1, 1),))] * 2,
        compiler_params=pltpu.CompilerParams(
            collective_id=0, has_side_effects=True, vmem_limit_bytes=48 * 1024 * 1024
        ),
    )(
        positions, species[None], cell_map, neighbours, struct_ids[None], embed, w_up,
        w_rad_in, w_rad_out, w_mix, read_first[None], read_hidden, read_last[None],
    )
    return energies[0], virials, forces


def solution(mesh):
    counts = tuple(mesh.shape[axis] for axis in AXES)
    return jax.shard_map(
        functools.partial(shards, counts),
        mesh=mesh,
        in_specs=(P(None, AXES), P(AXES), P(AXES, None), P(None, AXES), P(AXES))
        + (P(),) * 8,
        out_specs=(P(), P(), P(None, AXES)),
        check_vma=False,
    )
```

```python
import functools
import math

import jax
import jax.numpy as jnp
from jax import lax
from jax.experimental import pallas as pl
from jax.experimental.pallas import tpu as pltpu
from jax.sharding import PartitionSpec as P

SLAB_STRUCTS = 4
AXES = ("gx", "gy", "gz")
MESH = pl.DeviceIdType.MESH
cutoff = 6.0
box_side = 4.5
soften = 0.25
f32 = jnp.float32
bf16 = jnp.bfloat16


def split2(x):
    high = x.astype(bf16)
    return high, (x - high.astype(f32)).astype(bf16)


def parts3(x):
    high = x.astype(bf16).astype(f32)
    rest = x - high
    mid = rest.astype(bf16).astype(f32)
    return jnp.concatenate([high, mid, rest - mid], axis=0)


def dot(left, right, dims):
    return lax.dot_general(
        left, right, (((dims[0],), (dims[1],)), ((), ())), preferred_element_type=f32
    )


def dot3(left, right, dims):
    lh, ll = split2(left)
    rh, rl = split2(right)
    return dot(lh, rh, dims) + (dot(lh, rl, dims) + dot(ll, rh, dims))


def dot3_tall(left, right):
    lh = left.astype(bf16).astype(f32)
    rh = right.astype(bf16).astype(f32)
    lefts = jnp.concatenate([lh, lh, left - lh], axis=0).astype(bf16)
    rights = jnp.concatenate([rh, right - rh, rh], axis=0).astype(bf16)
    return dot(lefts, rights, (0, 0))


def pick(table, chosen):
    width = table.shape[0]
    both = dot(jnp.concatenate(split2(table), axis=0), chosen, (1, 0))
    return both[:width] + both[width:]


def to_col(row):
    n = row.shape[1]
    same = lax.broadcasted_iota(jnp.int32, (n, n), 0) == lax.broadcasted_iota(jnp.int32, (n, n), 1)
    return jnp.sum(jnp.where(same, jnp.broadcast_to(row, (n, n)), 0.0), axis=1, keepdims=True)


def sigmoid(x):
    return 1.0 / (1.0 + jnp.exp(-x))


def sin_cos_pi(turns):
    near = jnp.floor(turns + 0.5)
    x = (turns - near) * math.pi
    sign = 1.0 - 2.0 * (near - 2.0 * jnp.floor(near * 0.5))
    x2 = x * x
    s = jnp.full_like(x, 1.0 / math.factorial(13))
    for p in (11, 9, 7, 5, 3, 1):
        s = s * x2 + (-1.0) ** ((p - 1) // 2) / math.factorial(p)
    c = jnp.full_like(x, 1.0 / math.factorial(12))
    for p in (10, 8, 6, 4, 2, 0):
        c = c * x2 + (-1.0) ** (p // 2) / math.factorial(p)
    return s * x * sign, c * sign


def kernel(
    counts,
    *refs,
):
    inputs, outer = refs[:13], refs[13:]
    run(counts, inputs, *outer)


def run(
    counts, inputs,
    en_out, vir_out, f_out,
    stage, emb, oh, soh, dirs, pre, rad, picked, grads, d_rad, d_pick, ddir, feats,
    sendp, sends, recvp, reccs, lsend, tables, back, backs, fsend, frecv, red, redstage,
    slab_buf, gx_send, gx_buf,
    pos, spe, cmap, nbr, sid, embed, w_up, w_ri, w_ro, w_mix, rfirst, rhid, rlast, in_s,
    p_s, p_r, s_s, s_r, l_s, l_r, b_s, b_r, f_s, f_r, a_s, a_r, g_s, g_r,
):
    held = (pos, spe, cmap, nbr, sid, embed, w_up, w_ri, w_ro, w_mix, rfirst, rhid, rlast)
    loads = [pltpu.make_async_copy(src, dst, in_s.at[i]) for i, (src, dst) in enumerate(zip(inputs, held))]
    for i in (3, 0, 1, 2, 4, 5, 6, 9, 8, 7, 10, 11, 12):
        loads[i].start()
    nx, ny, nz = counts
    size = dict(zip(AXES, counts))
    me = {axis: lax.axis_index(axis) for axis in AXES}
    atoms = pos.shape[1]
    neigh = nbr.shape[0]
    edges = neigh * atoms
    chans = embed.shape[1]
    per_cell = atoms // 8
    scaling = 1.0 / math.sqrt(neigh)

    def at(shift):
        return {
            axis: lax.rem(me[axis] + (step % size[axis]), size[axis])
            for axis, step in zip(AXES, shift)
            if step % size[axis]
        }

    slab_shifts = [(0, j, k) for j in range(ny) for k in range(nz) if (j, k) != (0, 0)]
    gx_shifts = [(i, 0, 0) for i in range(1, nx)]
    peers = slab_shifts + gx_shifts
    barrier = pltpu.get_barrier_semaphore()
    for shift in peers:
        pl.semaphore_signal(barrier, inc=1, device_id=at(shift), device_id_type=MESH)

    def face_shift(axis, step):
        return tuple(step if a == axis else 0 for a in range(3))

    def remote(src, dst, send, recv, shift):
        return pltpu.make_async_remote_copy(
            src_ref=src, dst_ref=dst, send_sem=send, recv_sem=recv,
            device_id=at(shift), device_id_type=MESH,
        )

    stage[...] = jnp.zeros_like(stage)
    for load in loads[:5]:
        load.wait()
    stage[0:neigh, :] = nbr[...].astype(f32)
    base = stage.shape[0] - 8
    stage[base : base + 3, :] = pos[...]
    stage[base + 3 : base + 4, :] = spe[...].astype(f32)
    stage[base + 4 : base + 5, :] = sid[...].astype(f32)
    iota0 = lax.broadcasted_iota(jnp.int32, (atoms, atoms), 0)
    iota1 = lax.broadcasted_iota(jnp.int32, (atoms, atoms), 1)
    cm_row = cmap[...]
    order_t = jnp.where(iota0 == cm_row, 1.0, 0.0).astype(bf16)
    height = stage.shape[0]
    moved = dot(parts3(stage[...]).astype(bf16), order_t, (1, 0))
    moved = moved[:height] + moved[height : 2 * height] + moved[2 * height :]
    nbr_c = moved[0:neigh].astype(jnp.int32)
    tail = moved[base : base + 8]
    row8 = lax.broadcasted_iota(jnp.int32, (8, atoms), 0)
    pos_c = jnp.where(row8 < 3, tail, 0.0)
    spe_c = tail[3:4].astype(jnp.int32)
    sid_c = tail[4:5].astype(jnp.int32)
    sendp[...] = pos_c
    sends[...] = jnp.broadcast_to(spe_c, (8, atoms))

    pl.semaphore_wait(barrier, len(peers))
    copies = []
    for axis in range(3):
        for face, step in ((2 * axis, 1), (2 * axis + 1, -1)):
            copies.append(remote(sendp, recvp.at[face], p_s.at[face], p_r.at[face], face_shift(axis, step)))
            copies.append(remote(sends, reccs.at[face], s_s.at[face], s_r.at[face], face_shift(axis, step)))
    for copy in copies:
        copy.start()

    cm_col = to_col(cm_row.astype(f32)).astype(jnp.int32)
    own_slot = jnp.broadcast_to(cm_col, (atoms, atoms))
    half = atoms // 2
    bits = [(iota0 // (per_cell * w)) % 2 for w in (4, 2, 1)]
    inner = iota0 % per_cell
    ids = [own_slot]
    for axis in range(3):
        others = [bits[a] for a in range(3) if a != axis]
        ids.append(
            (axis + 1) * atoms + (1 - bits[axis]) * half
            + others[0] * (2 * per_cell) + others[1] * per_cell + inner
        )
    for t in range(4):
        for k in range(neigh):
            oh[t * atoms : (t + 1) * atoms, k * atoms : (k + 1) * atoms] = jnp.where(
                ids[t] == nbr_c[k : k + 1], 1.0, 0.0
            ).astype(bf16)
    for load in loads[5:]:
        load.wait()
    elements = embed.shape[0]
    emb[...] = jnp.zeros_like(emb)
    emb[0:elements, :] = embed[...]
    table = emb[...]
    lifted_zero = dot3(table, w_up[0], (1, 0)).T
    el_iota = lax.broadcasted_iota(jnp.int32, (table.shape[0], atoms), 0)
    own_el = jnp.where(el_iota == spe_c, 1.0, 0.0).astype(bf16)
    initial = pick(table.T, own_el)
    first_col = to_col(rfirst[...])
    last_col = to_col(rlast[...])

    for copy in copies:
        copy.wait()

    lane_bits = [(lax.broadcasted_iota(jnp.int32, (8, atoms), 1) // (per_cell * w)) % 2 for w in (4, 2, 1)]
    pieces = [jnp.where(row8 == 3, jnp.broadcast_to(spe_c, (8, atoms)).astype(f32), pos_c)]
    for axis in range(3):
        low = lane_bits[axis] == 1
        where_pos = jnp.where(low, recvp[2 * axis], recvp[2 * axis + 1])
        shifted = where_pos + jnp.where(low, -box_side, box_side)
        where_pos = jnp.where(row8 == axis, shifted, where_pos)
        where_el = jnp.where(low, reccs[2 * axis], reccs[2 * axis + 1]).astype(f32)
        pieces.append(jnp.where(row8 == 3, where_el, where_pos))
    ext = jnp.concatenate(pieces, axis=1)
    ext3 = jnp.concatenate([parts3(ext), jnp.zeros_like(ext)], axis=0).astype(bf16)
    far = dot(ext3, oh[...], (1, 0))
    far = far[0:8] + far[8:16] + far[16:24]
    ev = far - jnp.concatenate([pos_c] * neigh, axis=1)
    far_el = far[3:4].astype(jnp.int32)
    for k in range(neigh):
        cols = slice(k * atoms, (k + 1) * atoms)
        soh[:, cols] = jnp.where(el_iota == far_el[:, cols], 1.0, 0.0).astype(bf16)
    r2 = ev[0:1] * ev[0:1] + ev[1:2] * ev[1:2] + ev[2:3] * ev[2:3]
    radius = jnp.sqrt(r2 + soften)
    inv = 1.0 / radius
    room = jnp.maximum(0.0, 1.0 - radius * radius / (cutoff * cutoff))
    env = room * room
    d_env = room * radius * (-4.0 / (cutoff * cutoff))
    bessels = w_ri.shape[1]
    harm = (lax.broadcasted_iota(jnp.int32, (bessels, edges), 0) + 1).astype(f32)
    sn, cs = sin_cos_pi(harm * (radius * (1.0 / cutoff)))
    amp = math.sqrt(2.0 / cutoff) * inv
    bessel = sn * (amp * env)
    d_bessel = amp * (env * (harm * (math.pi / cutoff) * cs - sn * inv) + sn * d_env)
    dirs[...] = ev * inv

    chunk = 32

    def radial(layer):
        x = dot3_tall(w_ri[layer], bessel)
        pre[layer] = x
        rad[layer] = dot3_tall(w_ro[layer], x * sigmoid(x))

    def forward(layer):
        for c in range(0, chans, chunk):
            s = v0 = v1 = v2 = None
            for k in range(neigh):
                cols = pl.ds(k * atoms, atoms)
                p = picked[layer, pl.ds(c, chunk), cols]
                a = rad[layer, pl.ds(c, chunk), cols] * p
                b = rad[layer, pl.ds(chans + c, chunk), cols] * p
                d = [dirs[pl.ds(m, 1), cols] for m in range(3)]
                if k == 0:
                    s, v0, v1, v2 = a, d[0] * b, d[1] * b, d[2] * b
                else:
                    s, v0, v1, v2 = s + a, v0 + d[0] * b, v1 + d[1] * b, v2 + d[2] * b
            s = s * scaling
            vs = [v * scaling for v in (v0, v1, v2)]
            rows = pl.ds(c, chunk)
            for m in range(3):
                feats[layer, 3 + m, rows, :] = vs[m]
            feats[layer, 0, rows, :] = s
            feats[layer, 1, rows, :] = vs[0] * vs[0] + vs[1] * vs[1] + vs[2] * vs[2]
            feats[layer, 2, rows, :] = s * s
        stacked = feats[layer, 0:3].reshape(3 * chans, atoms)
        return dot3(w_mix[layer].reshape(3 * chans, chans), stacked, (0, 0))

    def backward(layer, d_mix, with_pick):
        d_st = dot3(w_mix[layer].reshape(3 * chans, chans), d_mix, (1, 0))
        d_s = d_st[0:chans] + 2.0 * feats[layer, 0] * d_st[2 * chans :]
        grads[0] = d_s * scaling
        twice = d_st[chans : 2 * chans] * (2.0 * scaling)
        for m in range(3):
            grads[1 + m] = feats[layer, 3 + m] * twice
        for k in range(neigh):
            cols = pl.ds(k * atoms, atoms)
            d = [dirs[pl.ds(m, 1), cols] for m in range(3)]
            acc = [jnp.zeros((8, atoms), f32)] * 3
            for c in range(0, chans, chunk):
                rows = pl.ds(c, chunk)
                g = [grads[m, rows, :] for m in range(4)]
                p = picked[layer, rows, cols]
                b = rad[layer, pl.ds(chans + c, chunk), cols]
                t = d[0] * g[1] + d[1] * g[2] + d[2] * g[3]
                d_rad[rows, cols] = g[0] * p
                d_rad[pl.ds(chans + c, chunk), cols] = t * p
                if with_pick:
                    d_pick[rows, cols] = g[0] * rad[layer, rows, cols] + t * b
                q = b * p
                acc = [
                    acc[m] + jnp.sum((g[1 + m] * q).reshape(chunk // 8, 8, atoms), axis=0)
                    for m in range(3)
                ]
            for m in range(3):
                ddir[layer, pl.ds(m, 1), cols] = jnp.sum(acc[m], axis=0, keepdims=True)

    def backward_radial(layer):
        d_hidden = dot3(w_ro[layer], d_rad[...], (1, 0))
        x = pre[layer]
        sig = sigmoid(x)
        return dot3(w_ri[layer], d_hidden * sig * (1.0 + x * (1.0 - sig)), (1, 0))

    ddir[...] = jnp.zeros_like(ddir)
    radial(0)
    picked[0] = pick(lifted_zero, soh[...])
    layer_out = initial + forward(0)
    lifted = dot3(layer_out, w_up[1], (0, 0))
    grid = (2, 2, 2, per_cell, chans)
    lsend[...] = lifted.reshape(grid)

    def part(ref, axis, side):
        return ref.at[(slice(None),) * axis + (side,)]

    copies = []
    for axis in range(3):
        for side, step in ((1, 1), (0, -1)):
            i = 2 * axis + side
            copies.append(
                remote(part(lsend, axis, side), part(tables.at[axis], axis, side), l_s.at[i], l_r.at[i], face_shift(axis, step))
            )
    for copy in copies:
        copy.start()
    radial(1)
    own_pick = pick(lifted.T, oh[0:atoms, :])
    for copy in copies:
        copy.wait()
    ghosts = jnp.concatenate([tables[a].reshape(atoms, chans).T for a in range(3)], axis=1)
    picked[1] = own_pick + pick(ghosts, oh[atoms:, :])
    second = layer_out + forward(1)
    x2 = dot3(rhid[...], second, (1, 0))
    sig2 = sigmoid(x2)
    energy = jnp.sum(first_col * layer_out, axis=0, keepdims=True) + jnp.sum(
        last_col * (x2 * sig2), axis=0, keepdims=True
    )
    d_second = dot3(rhid[...], last_col * (sig2 * (1.0 + x2 * (1.0 - sig2))), (0, 0))
    backward(1, d_second, True)
    d_ext = dot(oh[...], jnp.concatenate(split2(d_pick[...]), axis=0), (1, 1))
    d_ext = d_ext[:, :chans] + d_ext[:, chans:]
    for axis in range(3):
        back[axis] = d_ext[(axis + 1) * atoms : (axis + 2) * atoms].reshape(grid)
    copies = []
    for axis in range(3):
        for side, step in ((1, -1), (0, 1)):
            i = 2 * axis + side
            copies.append(
                remote(part(back.at[axis], axis, side), part(backs.at[axis], axis, side), b_s.at[i], b_r.at[i], face_shift(axis, step))
            )
    for copy in copies:
        copy.start()
    d_bes = backward_radial(1)
    for copy in copies:
        copy.wait()
    d_lifted = d_ext[0:atoms]
    for axis in range(3):
        d_lifted = d_lifted + backs[axis].reshape(atoms, chans)
    d_layer = d_second + first_col + dot3(w_up[1], d_lifted, (1, 1))
    backward(0, d_layer, False)
    d_bes = d_bes + backward_radial(0)
    d_dir = ddir[0] + ddir[1]
    along = d_dir * ev
    d_radius = jnp.sum(d_bes * d_bessel, axis=0, keepdims=True) - (
        along[0:1] + along[1:2] + along[2:3]
    ) * (inv * inv)
    edge_row = lax.broadcasted_iota(jnp.int32, (8, edges), 0)
    eg = jnp.where(edge_row < 3, d_dir * inv + ev * (d_radius * inv), 0.0)

    redstage[...] = jnp.zeros_like(redstage)

    def over_slots(x):
        total = x[:, 0:atoms]
        for k in range(1, neigh):
            total = total + x[:, k * atoms : (k + 1) * atoms]
        return total

    for r in range(3):
        redstage[3 * r : 3 * r + 3, :] = -over_slots(ev[r : r + 1] * eg)[0:3]
    redstage[9:10, :] = energy
    structs = SLAB_STRUCTS * nx
    member = jnp.where(
        lax.broadcasted_iota(jnp.int32, (structs, atoms), 0) == sid_c, 1.0, 0.0
    ).astype(bf16)
    shares = dot(parts3(redstage[...]).astype(bf16), member, (1, 1))
    shares = shares[0:16] + shares[16:32] + shares[32:48]
    red[...] = shares
    my_slot = me["gy"] * nz + me["gz"]
    sums = []
    for i, shift in enumerate(slab_shifts):
        sums.append(remote(red, slab_buf.at[my_slot], a_s.at[i], a_r.at[i], shift))
    for copy in sums:
        copy.start()

    eg3 = jnp.concatenate([parts3(eg), jnp.zeros_like(eg)], axis=0).astype(bf16)
    spread = dot(eg3, oh[...], (1, 1))
    spread = spread[0:8] + spread[8:16] + spread[16:24]
    for axis in range(3):
        fsend[axis] = spread[:, (axis + 1) * atoms : (axis + 2) * atoms]
    copies = []
    for axis in range(3):
        for face, step in ((2 * axis, -1), (2 * axis + 1, 1)):
            copies.append(remote(fsend.at[axis], frecv.at[face], f_s.at[face], f_r.at[face], face_shift(axis, step)))
    for copy in copies:
        copy.start()
    own = spread[:, 0:atoms] - over_slots(eg)
    slab_buf[my_slot] = red[...]
    for copy in sums:
        copy.wait()
    total = slab_buf[0]
    for i in range(1, ny * nz):
        total = total + slab_buf[i]
    gx_send[...] = total
    sums = []
    for i, shift in enumerate(gx_shifts):
        sums.append(remote(gx_send, gx_buf.at[i], g_s.at[i], g_r.at[i], shift))
    for copy in sums:
        copy.start()
    for copy in copies:
        copy.wait()
    for axis in range(3):
        own = own + jnp.where(lane_bits[axis] == 1, frecv[2 * axis], frecv[2 * axis + 1])
    order = jnp.where(own_slot == iota1, 1.0, 0.0).astype(bf16)
    own3 = jnp.concatenate([parts3(-own), jnp.zeros_like(own)], axis=0).astype(bf16)
    forces = dot(own3, order, (1, 0))
    f_out[...] = (forces[0:8] + forces[8:16] + forces[16:24])[0:3]
    for copy in sums:
        copy.wait()
    for i in range(len(gx_shifts)):
        total = total + gx_buf[i]
    vir_out[...] = total[0:9]
    en_out[...] = total[9:10]


def shards(counts, *args):
    (positions, species, cell_map, neighbours, struct_ids, embed, w_up, w_rad_in, w_rad_out,
     w_mix, read_first, read_hidden, read_last) = args
    nx, ny, nz = counts
    atoms = positions.shape[1]
    neigh = neighbours.shape[0]
    edges = neigh * atoms
    chans = embed.shape[1]
    hidden = w_rad_in.shape[2]
    per_cell = atoms // 8
    structs = SLAB_STRUCTS * nx
    el_rows = -(-embed.shape[0] // 128) * 128
    grid = (2, 2, 2, per_cell, chans)
    operands = (
        positions, species[None], cell_map, neighbours, struct_ids[None], embed, w_up,
        w_rad_in, w_rad_out, w_mix, read_first[None], read_hidden.T, read_last[None],
    )
    dma = pltpu.SemaphoreType.DMA
    vm = lambda *shape: pltpu.VMEM(shape, f32)
    vmem = pl.BlockSpec(memory_space=pltpu.VMEM)
    energies, virials, forces = pl.pallas_call(
        functools.partial(kernel, counts),
        out_shape=(
            jax.ShapeDtypeStruct((1, structs), f32),
            jax.ShapeDtypeStruct((9, structs), f32),
            jax.ShapeDtypeStruct((3, atoms), f32),
        ),
        in_specs=[pl.BlockSpec(memory_space=pltpu.HBM)] * 13,
        out_specs=(vmem, vmem, vmem),
        scratch_shapes=[
            vm(-(-neigh // 8) * 8 + 8, atoms),
            vm(el_rows, chans),
            pltpu.VMEM((4 * atoms, edges), bf16),
            pltpu.VMEM((el_rows, edges), bf16),
            vm(8, edges),
            vm(2, hidden, edges),
            vm(2, 2 * chans, edges),
            vm(2, chans, edges),
            vm(4, chans, atoms),
            vm(2 * chans, edges),
            vm(chans, edges),
            vm(2, 8, edges),
            vm(2, 6, chans, atoms),
            vm(8, atoms),
            pltpu.VMEM((8, atoms), jnp.int32),
            vm(6, 8, atoms),
            pltpu.VMEM((6, 8, atoms), jnp.int32),
            vm(*grid),
            vm(3, *grid),
            vm(3, *grid),
            vm(3, *grid),
            vm(3, 8, atoms),
            vm(6, 8, atoms),
            vm(16, structs),
            vm(16, atoms),
            vm(ny * nz, 16, structs),
            vm(16, structs),
            vm(max(nx - 1, 1), 16, structs),
        ]
        + [pltpu.VMEM(x.shape, x.dtype) for x in operands]
        + [dma((13,))]
        + [dma((6,))] * 10
        + [dma((ny * nz - 1,))] * 2
        + [dma((max(nx - 1, 1),))] * 2,
        compiler_params=pltpu.CompilerParams(
            collective_id=0, has_side_effects=True, vmem_limit_bytes=48 * 1024 * 1024
        ),
    )(*operands)
    return energies[0], virials, forces


def solution(mesh):
    counts = tuple(mesh.shape[axis] for axis in AXES)
    return jax.shard_map(
        functools.partial(shards, counts),
        mesh=mesh,
        in_specs=(P(None, AXES), P(AXES), P(AXES, None), P(None, AXES), P(AXES))
        + (P(),) * 8,
        out_specs=(P(), P(), P(None, AXES)),
        check_vma=False,
    )
```

```python
import functools
import math

import jax
import jax.numpy as jnp
from jax import lax
from jax.experimental import pallas as pl
from jax.experimental.pallas import tpu as pltpu
from jax.sharding import PartitionSpec as P

SLAB_STRUCTS = 4
AXES = ("gx", "gy", "gz")
MESH = pl.DeviceIdType.MESH
cutoff = 6.0
box_side = 4.5
soften = 0.25
f32 = jnp.float32
bf16 = jnp.bfloat16


def split2(x):
    high = x.astype(bf16)
    return high, (x - high.astype(f32)).astype(bf16)


def parts3(x):
    high = x.astype(bf16).astype(f32)
    rest = x - high
    mid = rest.astype(bf16).astype(f32)
    return jnp.concatenate([high, mid, rest - mid], axis=0)


def dot(left, right, dims):
    return lax.dot_general(
        left, right, (((dims[0],), (dims[1],)), ((), ())), preferred_element_type=f32
    )


def dot3(left, right, dims):
    lh, ll = split2(left)
    rh, rl = split2(right)
    return dot(lh, rh, dims) + (dot(lh, rl, dims) + dot(ll, rh, dims))


def dot3_tall(left, right):
    lh = left.astype(bf16).astype(f32)
    rh = right.astype(bf16).astype(f32)
    lefts = jnp.concatenate([lh, lh, left - lh], axis=0).astype(bf16)
    rights = jnp.concatenate([rh, right - rh, rh], axis=0).astype(bf16)
    return dot(lefts, rights, (0, 0))


def pick(table, chosen):
    width = table.shape[0]
    both = dot(jnp.concatenate(split2(table), axis=0), chosen, (1, 0))
    return both[:width] + both[width:]


def to_col(row):
    n = row.shape[1]
    same = lax.broadcasted_iota(jnp.int32, (n, n), 0) == lax.broadcasted_iota(jnp.int32, (n, n), 1)
    return jnp.sum(jnp.where(same, jnp.broadcast_to(row, (n, n)), 0.0), axis=1, keepdims=True)


def sigmoid(x):
    return 1.0 / (1.0 + jnp.exp(-x))


def sin_cos_pi(turns):
    near = jnp.floor(turns + 0.5)
    x = (turns - near) * math.pi
    sign = 1.0 - 2.0 * (near - 2.0 * jnp.floor(near * 0.5))
    x2 = x * x
    s = jnp.full_like(x, 1.0 / math.factorial(13))
    for p in (11, 9, 7, 5, 3, 1):
        s = s * x2 + (-1.0) ** ((p - 1) // 2) / math.factorial(p)
    c = jnp.full_like(x, 1.0 / math.factorial(12))
    for p in (10, 8, 6, 4, 2, 0):
        c = c * x2 + (-1.0) ** (p // 2) / math.factorial(p)
    return s * x * sign, c * sign


def kernel(
    counts,
    *refs,
):
    inputs, outer = refs[:13], refs[13:]
    run(counts, inputs, *outer)


def run(
    counts, inputs,
    packed,
    stage, emb, oh, soh, dirs, pre, rad, picked, grads, d_rad, d_pick, ddir, feats,
    sendp, sends, recvp, reccs, lsend, tables, back, backs, fsend, frecv, red, redstage,
    slab_buf, gx_send, gx_buf,
    pos, spe, cmap, nbr, sid, embed, w_up, w_ri, w_ro, w_mix, rfirst, rhid, rlast, in_s,
    p_s, p_r, s_s, s_r, l_s, l_r, b_s, b_r, f_s, f_r, a_s, a_r, g_s, g_r,
):
    held = (pos, spe, cmap, nbr, sid, embed, w_up, w_ri, w_ro, w_mix, rfirst, rhid, rlast)
    loads = [pltpu.make_async_copy(src, dst, in_s.at[i]) for i, (src, dst) in enumerate(zip(inputs, held))]
    for i in (3, 0, 1, 2, 4, 5, 6, 9, 8, 7, 10, 11, 12):
        loads[i].start()
    nx, ny, nz = counts
    size = dict(zip(AXES, counts))
    me = {axis: lax.axis_index(axis) for axis in AXES}
    atoms = pos.shape[1]
    neigh = nbr.shape[0]
    edges = neigh * atoms
    chans = embed.shape[1]
    per_cell = atoms // 8
    scaling = 1.0 / math.sqrt(neigh)

    def at(shift):
        return {
            axis: lax.rem(me[axis] + (step % size[axis]), size[axis])
            for axis, step in zip(AXES, shift)
            if step % size[axis]
        }

    slab_shifts = [(0, j, k) for j in range(ny) for k in range(nz) if (j, k) != (0, 0)]
    gx_shifts = [(i, 0, 0) for i in range(1, nx)]
    one_step = in_one_step(counts)
    all_shifts = [
        (i, j, k) for i in range(nx) for j in range(ny) for k in range(nz) if (i, j, k) != (0, 0, 0)
    ]
    peers = all_shifts if one_step else slab_shifts + gx_shifts
    barrier = pltpu.get_barrier_semaphore()
    for shift in peers:
        pl.semaphore_signal(barrier, inc=1, device_id=at(shift), device_id_type=MESH)

    def face_shift(axis, step):
        return tuple(step if a == axis else 0 for a in range(3))

    def remote(src, dst, send, recv, shift):
        return pltpu.make_async_remote_copy(
            src_ref=src, dst_ref=dst, send_sem=send, recv_sem=recv,
            device_id=at(shift), device_id_type=MESH,
        )

    stage[...] = jnp.zeros_like(stage)
    for load in loads[:5]:
        load.wait()
    stage[0:neigh, :] = nbr[...].astype(f32)
    base = stage.shape[0] - 8
    stage[base : base + 3, :] = pos[...]
    stage[base + 3 : base + 4, :] = spe[...].astype(f32)
    stage[base + 4 : base + 5, :] = sid[...].astype(f32)
    iota0 = lax.broadcasted_iota(jnp.int32, (atoms, atoms), 0)
    iota1 = lax.broadcasted_iota(jnp.int32, (atoms, atoms), 1)
    cm_row = cmap[...]
    order_t = jnp.where(iota0 == cm_row, 1.0, 0.0).astype(bf16)
    height = stage.shape[0]
    moved = dot(parts3(stage[...]).astype(bf16), order_t, (1, 0))
    moved = moved[:height] + moved[height : 2 * height] + moved[2 * height :]
    nbr_c = moved[0:neigh].astype(jnp.int32)
    tail = moved[base : base + 8]
    row8 = lax.broadcasted_iota(jnp.int32, (8, atoms), 0)
    pos_c = jnp.where(row8 < 3, tail, 0.0)
    spe_c = tail[3:4].astype(jnp.int32)
    sid_c = tail[4:5].astype(jnp.int32)
    sendp[...] = pos_c
    sends[...] = jnp.broadcast_to(spe_c, (8, atoms))

    pl.semaphore_wait(barrier, len(peers))
    copies = []
    for axis in range(3):
        for face, step in ((2 * axis, 1), (2 * axis + 1, -1)):
            copies.append(remote(sendp, recvp.at[face], p_s.at[face], p_r.at[face], face_shift(axis, step)))
            copies.append(remote(sends, reccs.at[face], s_s.at[face], s_r.at[face], face_shift(axis, step)))
    for copy in copies:
        copy.start()

    cm_col = to_col(cm_row.astype(f32)).astype(jnp.int32)
    own_slot = jnp.broadcast_to(cm_col, (atoms, atoms))
    half = atoms // 2
    bits = [(iota0 // (per_cell * w)) % 2 for w in (4, 2, 1)]
    inner = iota0 % per_cell
    ids = [own_slot]
    for axis in range(3):
        others = [bits[a] for a in range(3) if a != axis]
        ids.append(
            (axis + 1) * atoms + (1 - bits[axis]) * half
            + others[0] * (2 * per_cell) + others[1] * per_cell + inner
        )
    for t in range(4):
        for k in range(neigh):
            oh[t * atoms : (t + 1) * atoms, k * atoms : (k + 1) * atoms] = jnp.where(
                ids[t] == nbr_c[k : k + 1], 1.0, 0.0
            ).astype(bf16)
    for load in loads[5:]:
        load.wait()
    elements = embed.shape[0]
    emb[...] = jnp.zeros_like(emb)
    emb[0:elements, :] = embed[...]
    table = emb[...]
    lifted_zero = dot3(table, w_up[0], (1, 0)).T
    el_iota = lax.broadcasted_iota(jnp.int32, (table.shape[0], atoms), 0)
    own_el = jnp.where(el_iota == spe_c, 1.0, 0.0).astype(bf16)
    initial = pick(table.T, own_el)
    first_col = to_col(rfirst[...])
    last_col = to_col(rlast[...])

    for copy in copies:
        copy.wait()

    lane_bits = [(lax.broadcasted_iota(jnp.int32, (8, atoms), 1) // (per_cell * w)) % 2 for w in (4, 2, 1)]
    pieces = [jnp.where(row8 == 3, jnp.broadcast_to(spe_c, (8, atoms)).astype(f32), pos_c)]
    for axis in range(3):
        low = lane_bits[axis] == 1
        where_pos = jnp.where(low, recvp[2 * axis], recvp[2 * axis + 1])
        shifted = where_pos + jnp.where(low, -box_side, box_side)
        where_pos = jnp.where(row8 == axis, shifted, where_pos)
        where_el = jnp.where(low, reccs[2 * axis], reccs[2 * axis + 1]).astype(f32)
        pieces.append(jnp.where(row8 == 3, where_el, where_pos))
    ext = jnp.concatenate(pieces, axis=1)
    ext3 = jnp.concatenate([parts3(ext), jnp.zeros_like(ext)], axis=0).astype(bf16)
    far = dot(ext3, oh[...], (1, 0))
    far = far[0:8] + far[8:16] + far[16:24]
    ev = far - jnp.concatenate([pos_c] * neigh, axis=1)
    far_el = far[3:4].astype(jnp.int32)
    for k in range(neigh):
        cols = slice(k * atoms, (k + 1) * atoms)
        soh[:, cols] = jnp.where(el_iota == far_el[:, cols], 1.0, 0.0).astype(bf16)
    r2 = ev[0:1] * ev[0:1] + ev[1:2] * ev[1:2] + ev[2:3] * ev[2:3]
    radius = jnp.sqrt(r2 + soften)
    inv = 1.0 / radius
    room = jnp.maximum(0.0, 1.0 - radius * radius / (cutoff * cutoff))
    env = room * room
    d_env = room * radius * (-4.0 / (cutoff * cutoff))
    bessels = w_ri.shape[1]
    harm = (lax.broadcasted_iota(jnp.int32, (bessels, edges), 0) + 1).astype(f32)
    sn, cs = sin_cos_pi(harm * (radius * (1.0 / cutoff)))
    amp = math.sqrt(2.0 / cutoff) * inv
    bessel = sn * (amp * env)
    d_bessel = amp * (env * (harm * (math.pi / cutoff) * cs - sn * inv) + sn * d_env)
    dirs[...] = ev * inv

    chunk = 32

    def radial(layer):
        x = dot3_tall(w_ri[layer], bessel)
        pre[layer] = x
        rad[layer] = dot3_tall(w_ro[layer], x * sigmoid(x))

    def forward(layer):
        for c in range(0, chans, chunk):
            s = v0 = v1 = v2 = None
            for k in range(neigh):
                cols = pl.ds(k * atoms, atoms)
                p = picked[layer, pl.ds(c, chunk), cols]
                a = rad[layer, pl.ds(c, chunk), cols] * p
                b = rad[layer, pl.ds(chans + c, chunk), cols] * p
                d = [dirs[pl.ds(m, 1), cols] for m in range(3)]
                if k == 0:
                    s, v0, v1, v2 = a, d[0] * b, d[1] * b, d[2] * b
                else:
                    s, v0, v1, v2 = s + a, v0 + d[0] * b, v1 + d[1] * b, v2 + d[2] * b
            s = s * scaling
            vs = [v * scaling for v in (v0, v1, v2)]
            rows = pl.ds(c, chunk)
            for m in range(3):
                feats[layer, 3 + m, rows, :] = vs[m]
            feats[layer, 0, rows, :] = s
            feats[layer, 1, rows, :] = vs[0] * vs[0] + vs[1] * vs[1] + vs[2] * vs[2]
            feats[layer, 2, rows, :] = s * s
        stacked = feats[layer, 0:3].reshape(3 * chans, atoms)
        return dot3(w_mix[layer].reshape(3 * chans, chans), stacked, (0, 0))

    def backward(layer, d_mix, with_pick):
        d_st = dot3(w_mix[layer].reshape(3 * chans, chans), d_mix, (1, 0))
        d_s = d_st[0:chans] + 2.0 * feats[layer, 0] * d_st[2 * chans :]
        grads[0] = d_s * scaling
        twice = d_st[chans : 2 * chans] * (2.0 * scaling)
        for m in range(3):
            grads[1 + m] = feats[layer, 3 + m] * twice
        for k in range(neigh):
            cols = pl.ds(k * atoms, atoms)
            d = [dirs[pl.ds(m, 1), cols] for m in range(3)]
            acc = [jnp.zeros((8, atoms), f32)] * 3
            for c in range(0, chans, chunk):
                rows = pl.ds(c, chunk)
                g = [grads[m, rows, :] for m in range(4)]
                p = picked[layer, rows, cols]
                b = rad[layer, pl.ds(chans + c, chunk), cols]
                t = d[0] * g[1] + d[1] * g[2] + d[2] * g[3]
                d_rad[rows, cols] = g[0] * p
                d_rad[pl.ds(chans + c, chunk), cols] = t * p
                if with_pick:
                    d_pick[rows, cols] = g[0] * rad[layer, rows, cols] + t * b
                q = b * p
                acc = [
                    acc[m] + jnp.sum((g[1 + m] * q).reshape(chunk // 8, 8, atoms), axis=0)
                    for m in range(3)
                ]
            for m in range(3):
                ddir[layer, pl.ds(m, 1), cols] = jnp.sum(acc[m], axis=0, keepdims=True)

    def backward_radial(layer):
        d_hidden = dot3(w_ro[layer], d_rad[...], (1, 0))
        x = pre[layer]
        sig = sigmoid(x)
        return dot3(w_ri[layer], d_hidden * sig * (1.0 + x * (1.0 - sig)), (1, 0))

    ddir[...] = jnp.zeros_like(ddir)
    radial(0)
    picked[0] = pick(lifted_zero, soh[...])
    layer_out = initial + forward(0)
    lifted = dot3(layer_out, w_up[1], (0, 0))
    grid = (2, 2, 2, per_cell, chans)
    lsend[...] = lifted.reshape(grid)

    def part(ref, axis, side):
        return ref.at[(slice(None),) * axis + (side,)]

    copies = []
    for axis in range(3):
        for side, step in ((1, 1), (0, -1)):
            i = 2 * axis + side
            copies.append(
                remote(part(lsend, axis, side), part(tables.at[axis], axis, side), l_s.at[i], l_r.at[i], face_shift(axis, step))
            )
    for copy in copies:
        copy.start()
    radial(1)
    own_pick = pick(lifted.T, oh[0:atoms, :])
    for copy in copies:
        copy.wait()
    ghosts = jnp.concatenate([tables[a].reshape(atoms, chans).T for a in range(3)], axis=1)
    picked[1] = own_pick + pick(ghosts, oh[atoms:, :])
    second = layer_out + forward(1)
    x2 = dot3(rhid[...], second, (1, 0))
    sig2 = sigmoid(x2)
    energy = jnp.sum(first_col * layer_out, axis=0, keepdims=True) + jnp.sum(
        last_col * (x2 * sig2), axis=0, keepdims=True
    )
    d_second = dot3(rhid[...], last_col * (sig2 * (1.0 + x2 * (1.0 - sig2))), (0, 0))
    backward(1, d_second, True)
    d_ext = dot(oh[...], jnp.concatenate(split2(d_pick[...]), axis=0), (1, 1))
    d_ext = d_ext[:, :chans] + d_ext[:, chans:]
    for axis in range(3):
        back[axis] = d_ext[(axis + 1) * atoms : (axis + 2) * atoms].reshape(grid)
    copies = []
    for axis in range(3):
        for side, step in ((1, -1), (0, 1)):
            i = 2 * axis + side
            copies.append(
                remote(part(back.at[axis], axis, side), part(backs.at[axis], axis, side), b_s.at[i], b_r.at[i], face_shift(axis, step))
            )
    for copy in copies:
        copy.start()
    d_bes = backward_radial(1)
    for copy in copies:
        copy.wait()
    d_lifted = d_ext[0:atoms]
    for axis in range(3):
        d_lifted = d_lifted + backs[axis].reshape(atoms, chans)
    d_layer = d_second + first_col + dot3(w_up[1], d_lifted, (1, 1))
    backward(0, d_layer, False)
    d_bes = d_bes + backward_radial(0)
    d_dir = ddir[0] + ddir[1]
    along = d_dir * ev
    d_radius = jnp.sum(d_bes * d_bessel, axis=0, keepdims=True) - (
        along[0:1] + along[1:2] + along[2:3]
    ) * (inv * inv)
    edge_row = lax.broadcasted_iota(jnp.int32, (8, edges), 0)
    eg = jnp.where(edge_row < 3, d_dir * inv + ev * (d_radius * inv), 0.0)

    redstage[...] = jnp.zeros_like(redstage)

    def over_slots(x):
        total = x[:, 0:atoms]
        for k in range(1, neigh):
            total = total + x[:, k * atoms : (k + 1) * atoms]
        return total

    for r in range(3):
        redstage[3 * r : 3 * r + 3, :] = -over_slots(ev[r : r + 1] * eg)[0:3]
    redstage[9:10, :] = energy
    structs = SLAB_STRUCTS * nx
    if one_step:
        slab_row = lax.broadcasted_iota(jnp.int32, (8, atoms), 0) + me["gx"] * SLAB_STRUCTS
        local = jnp.where(slab_row == sid_c, 1.0, 0.0).astype(bf16)
        shares = dot(local, parts3(redstage[...]).astype(bf16), (1, 1))
        shares = shares[:, 0:16] + shares[:, 16:32] + shares[:, 32:48]
        red[...] = shares[0:SLAB_STRUCTS]
        my_slot = (me["gx"] * ny + me["gy"]) * nz + me["gz"]
        first_shifts = all_shifts
    else:
        member = jnp.where(
            lax.broadcasted_iota(jnp.int32, (structs, atoms), 0) == sid_c, 1.0, 0.0
        ).astype(bf16)
        shares = dot(parts3(redstage[...]).astype(bf16), member, (1, 1))
        red[...] = shares[0:16] + shares[16:32] + shares[32:48]
        my_slot = me["gy"] * nz + me["gz"]
        first_shifts = slab_shifts
    sums = []
    for i, shift in enumerate(first_shifts):
        sums.append(remote(red, slab_buf.at[my_slot], a_s.at[i], a_r.at[i], shift))
    for copy in sums:
        copy.start()

    eg3 = jnp.concatenate([parts3(eg), jnp.zeros_like(eg)], axis=0).astype(bf16)
    spread = dot(eg3, oh[...], (1, 1))
    spread = spread[0:8] + spread[8:16] + spread[16:24]
    for axis in range(3):
        fsend[axis] = spread[:, (axis + 1) * atoms : (axis + 2) * atoms]
    copies = []
    for axis in range(3):
        for face, step in ((2 * axis, -1), (2 * axis + 1, 1)):
            copies.append(remote(fsend.at[axis], frecv.at[face], f_s.at[face], f_r.at[face], face_shift(axis, step)))
    for copy in copies:
        copy.start()
    own = spread[:, 0:atoms] - over_slots(eg)
    slab_buf[my_slot] = red[...]
    if not one_step:
        for copy in sums:
            copy.wait()
        total = slab_buf[0]
        for i in range(1, ny * nz):
            total = total + slab_buf[i]
        gx_send[...] = total
        sums = []
        for i, shift in enumerate(gx_shifts):
            sums.append(remote(gx_send, gx_buf.at[i], g_s.at[i], g_r.at[i], shift))
        for copy in sums:
            copy.start()
    for copy in copies:
        copy.wait()
    for axis in range(3):
        own = own + jnp.where(lane_bits[axis] == 1, frecv[2 * axis], frecv[2 * axis + 1])
    order = jnp.where(own_slot == iota1, 1.0, 0.0).astype(bf16)
    own3 = jnp.concatenate([parts3(-own), jnp.zeros_like(own)], axis=0).astype(bf16)
    forces = dot(own3, order, (1, 0))
    packed[16:19, 0:atoms] = (forces[0:8] + forces[8:16] + forces[16:24])[0:3]
    for copy in sums:
        copy.wait()
    if one_step:
        for g in range(nx):
            total = slab_buf[g * ny * nz]
            for i in range(1, ny * nz):
                total = total + slab_buf[g * ny * nz + i]
            gx_send[g * SLAB_STRUCTS : (g + 1) * SLAB_STRUCTS, :] = total
        total = gx_send[...].T
    else:
        for i in range(len(gx_shifts)):
            total = total + gx_buf[i]
    packed[0:16, 0:structs] = total


def in_one_step(counts):
    return math.prod(counts) <= 64


def unpack(packed, en_out, vir_out, f_out):
    structs = en_out.shape[1]
    en_out[...] = packed[9:10, 0:structs]
    vir_out[...] = packed[0:9, 0:structs]
    f_out[...] = packed[16:19, 0 : f_out.shape[1]]


def shards(counts, *args):
    (positions, species, cell_map, neighbours, struct_ids, embed, w_up, w_rad_in, w_rad_out,
     w_mix, read_first, read_hidden, read_last) = args
    nx, ny, nz = counts
    atoms = positions.shape[1]
    neigh = neighbours.shape[0]
    edges = neigh * atoms
    chans = embed.shape[1]
    hidden = w_rad_in.shape[2]
    per_cell = atoms // 8
    structs = SLAB_STRUCTS * nx
    el_rows = -(-embed.shape[0] // 128) * 128
    grid = (2, 2, 2, per_cell, chans)
    operands = (
        positions, species[None], cell_map, neighbours, struct_ids[None], embed, w_up,
        w_rad_in, w_rad_out, w_mix, read_first[None], read_hidden.T, read_last[None],
    )
    one_step = in_one_step(counts)
    share = (SLAB_STRUCTS, 16) if one_step else (16, structs)
    groups = nx * ny * nz if one_step else ny * nz
    dma = pltpu.SemaphoreType.DMA
    vm = lambda *shape: pltpu.VMEM(shape, f32)
    vmem = pl.BlockSpec(memory_space=pltpu.VMEM)
    packed = pl.pallas_call(
        functools.partial(kernel, counts),
        out_shape=jax.ShapeDtypeStruct((24, max(atoms, structs)), f32),
        in_specs=[pl.BlockSpec(memory_space=pltpu.HBM)] * 13,
        out_specs=vmem,
        scratch_shapes=[
            vm(-(-neigh // 8) * 8 + 8, atoms),
            vm(el_rows, chans),
            pltpu.VMEM((4 * atoms, edges), bf16),
            pltpu.VMEM((el_rows, edges), bf16),
            vm(8, edges),
            vm(2, hidden, edges),
            vm(2, 2 * chans, edges),
            vm(2, chans, edges),
            vm(4, chans, atoms),
            vm(2 * chans, edges),
            vm(chans, edges),
            vm(2, 8, edges),
            vm(2, 6, chans, atoms),
            vm(8, atoms),
            pltpu.VMEM((8, atoms), jnp.int32),
            vm(6, 8, atoms),
            pltpu.VMEM((6, 8, atoms), jnp.int32),
            vm(*grid),
            vm(3, *grid),
            vm(3, *grid),
            vm(3, *grid),
            vm(3, 8, atoms),
            vm(6, 8, atoms),
            vm(*share),
            vm(16, atoms),
            vm(groups, *share),
            vm(*((structs, 16) if one_step else share)),
            vm(max(nx - 1, 1), 16, structs),
        ]
        + [pltpu.VMEM(x.shape, x.dtype) for x in operands]
        + [dma((13,))]
        + [dma((6,))] * 10
        + [dma((groups - 1,))] * 2
        + [dma((max(nx - 1, 1),))] * 2,
        compiler_params=pltpu.CompilerParams(
            collective_id=0, has_side_effects=True, vmem_limit_bytes=60 * 1024 * 1024
        ),
    )(*operands)
    energies, virials, forces = pl.pallas_call(
        unpack,
        out_shape=(
            jax.ShapeDtypeStruct((1, structs), f32),
            jax.ShapeDtypeStruct((9, structs), f32),
            jax.ShapeDtypeStruct((3, atoms), f32),
        ),
        in_specs=[vmem],
        out_specs=(vmem, vmem, vmem),
        compiler_params=pltpu.CompilerParams(vmem_limit_bytes=60 * 1024 * 1024),
    )(packed)
    return energies[0], virials, forces


def solution(mesh):
    counts = tuple(mesh.shape[axis] for axis in AXES)
    return jax.shard_map(
        functools.partial(shards, counts),
        mesh=mesh,
        in_specs=(P(None, AXES), P(AXES), P(AXES, None), P(None, AXES), P(AXES))
        + (P(),) * 8,
        out_specs=(P(), P(), P(None, AXES)),
        check_vma=False,
    )
```

```python
import functools
import math

import jax
import jax.numpy as jnp
from jax import lax
from jax.experimental import pallas as pl
from jax.experimental.pallas import tpu as pltpu
from jax.sharding import PartitionSpec as P

SLAB_STRUCTS = 4
AXES = ("gx", "gy", "gz")
MESH = pl.DeviceIdType.MESH
cutoff = 6.0
box_side = 4.5
soften = 0.25
f32 = jnp.float32
bf16 = jnp.bfloat16


def split2(x):
    high = x.astype(bf16)
    return high, (x - high.astype(f32)).astype(bf16)


def parts3(x):
    high = x.astype(bf16).astype(f32)
    rest = x - high
    mid = rest.astype(bf16).astype(f32)
    return jnp.concatenate([high, mid, rest - mid], axis=0)


def dot(left, right, dims):
    return lax.dot_general(
        left, right, (((dims[0],), (dims[1],)), ((), ())), preferred_element_type=f32
    )


def dot3(left, right, dims):
    lh, ll = split2(left)
    rh, rl = split2(right)
    return dot(lh, rh, dims) + (dot(lh, rl, dims) + dot(ll, rh, dims))


def dot3_tall(left, right):
    lh = left.astype(bf16).astype(f32)
    rh = right.astype(bf16).astype(f32)
    lefts = jnp.concatenate([lh, lh, left - lh], axis=0).astype(bf16)
    rights = jnp.concatenate([rh, right - rh, rh], axis=0).astype(bf16)
    return dot(lefts, rights, (0, 0))


def pick(table, chosen):
    width = table.shape[0]
    both = dot(jnp.concatenate(split2(table), axis=0), chosen, (1, 0))
    return both[:width] + both[width:]


def to_col(row):
    n = row.shape[1]
    same = lax.broadcasted_iota(jnp.int32, (n, n), 0) == lax.broadcasted_iota(jnp.int32, (n, n), 1)
    return jnp.sum(jnp.where(same, jnp.broadcast_to(row, (n, n)), 0.0), axis=1, keepdims=True)


def sigmoid(x):
    return 1.0 / (1.0 + jnp.exp(-x))


def sin_cos_pi(turns):
    near = jnp.floor(turns + 0.5)
    x = (turns - near) * math.pi
    sign = 1.0 - 2.0 * (near - 2.0 * jnp.floor(near * 0.5))
    x2 = x * x
    s = jnp.full_like(x, 1.0 / math.factorial(13))
    for p in (11, 9, 7, 5, 3, 1):
        s = s * x2 + (-1.0) ** ((p - 1) // 2) / math.factorial(p)
    c = jnp.full_like(x, 1.0 / math.factorial(12))
    for p in (10, 8, 6, 4, 2, 0):
        c = c * x2 + (-1.0) ** (p // 2) / math.factorial(p)
    return s * x * sign, c * sign


def kernel(
    counts,
    *refs,
):
    inputs, outer = refs[:13], refs[13:]
    run(counts, inputs, *outer)


def run(
    counts, inputs,
    packed,
    stage, emb, oh, soh, dirs, pre, rad, picked, grads, d_rad, d_pick, ddir, feats,
    sendp, sends, recvp, reccs, lsend, tables, back, backs, fsend, frecv, red, redstage,
    slab_buf, gx_send, gx_buf,
    pos, spe, cmap, nbr, sid, embed, w_up, w_ri, w_ro, w_mix, rfirst, rhid, rlast, in_s,
    p_s, p_r, s_s, s_r, l_s, l_r, b_s, b_r, f_s, f_r, a_s, a_r, g_s, g_r,
):
    held = (pos, spe, cmap, nbr, sid, embed, w_up, w_ri, w_ro, w_mix, rfirst, rhid, rlast)
    loads = [pltpu.make_async_copy(src, dst, in_s.at[i]) for i, (src, dst) in enumerate(zip(inputs, held))]
    for i in (3, 0, 1, 2, 4, 5, 6, 9, 8, 7, 10, 11, 12):
        loads[i].start()
    nx, ny, nz = counts
    size = dict(zip(AXES, counts))
    me = {axis: lax.axis_index(axis) for axis in AXES}
    atoms = pos.shape[1]
    neigh = nbr.shape[0]
    edges = neigh * atoms
    chans = embed.shape[1]
    per_cell = atoms // 8
    scaling = 1.0 / math.sqrt(neigh)

    def at(shift):
        return {
            axis: lax.rem(me[axis] + (step % size[axis]), size[axis])
            for axis, step in zip(AXES, shift)
            if step % size[axis]
        }

    slab_shifts = [(0, j, k) for j in range(ny) for k in range(nz) if (j, k) != (0, 0)]
    gx_shifts = [(i, 0, 0) for i in range(1, nx)]
    one_step = in_one_step(counts)
    all_shifts = [
        (i, j, k) for i in range(nx) for j in range(ny) for k in range(nz) if (i, j, k) != (0, 0, 0)
    ]
    peers = all_shifts if one_step else slab_shifts + gx_shifts
    barrier = pltpu.get_barrier_semaphore()
    for shift in peers:
        pl.semaphore_signal(barrier, inc=1, device_id=at(shift), device_id_type=MESH)

    def face_shift(axis, step):
        return tuple(step if a == axis else 0 for a in range(3))

    def remote(src, dst, send, recv, shift):
        return pltpu.make_async_remote_copy(
            src_ref=src, dst_ref=dst, send_sem=send, recv_sem=recv,
            device_id=at(shift), device_id_type=MESH,
        )

    stage[...] = jnp.zeros_like(stage)
    for load in loads[:5]:
        load.wait()
    stage[0:neigh, :] = nbr[...].astype(f32)
    base = stage.shape[0] - 8
    stage[base : base + 3, :] = pos[...]
    stage[base + 3 : base + 4, :] = spe[...].astype(f32)
    stage[base + 4 : base + 5, :] = sid[...].astype(f32)
    iota0 = lax.broadcasted_iota(jnp.int32, (atoms, atoms), 0)
    iota1 = lax.broadcasted_iota(jnp.int32, (atoms, atoms), 1)
    cm_row = cmap[...]
    order_t = jnp.where(iota0 == cm_row, 1.0, 0.0).astype(bf16)
    height = stage.shape[0]
    moved = dot(parts3(stage[...]).astype(bf16), order_t, (1, 0))
    moved = moved[:height] + moved[height : 2 * height] + moved[2 * height :]
    nbr_c = moved[0:neigh].astype(jnp.int32)
    tail = moved[base : base + 8]
    row8 = lax.broadcasted_iota(jnp.int32, (8, atoms), 0)
    pos_c = jnp.where(row8 < 3, tail, 0.0)
    spe_c = tail[3:4].astype(jnp.int32)
    sid_c = tail[4:5].astype(jnp.int32)
    sendp[...] = pos_c
    sends[...] = jnp.broadcast_to(spe_c, (8, atoms))

    pl.semaphore_wait(barrier, len(peers))
    copies = []
    for axis in range(3):
        for face, step in ((2 * axis, 1), (2 * axis + 1, -1)):
            copies.append(remote(sendp, recvp.at[face], p_s.at[face], p_r.at[face], face_shift(axis, step)))
            copies.append(remote(sends, reccs.at[face], s_s.at[face], s_r.at[face], face_shift(axis, step)))
    for copy in copies:
        copy.start()

    cm_col = to_col(cm_row.astype(f32)).astype(jnp.int32)
    own_slot = jnp.broadcast_to(cm_col, (atoms, atoms))
    half = atoms // 2
    bits = [(iota0 // (per_cell * w)) % 2 for w in (4, 2, 1)]
    inner = iota0 % per_cell
    ids = [own_slot]
    for axis in range(3):
        others = [bits[a] for a in range(3) if a != axis]
        ids.append(
            (axis + 1) * atoms + (1 - bits[axis]) * half
            + others[0] * (2 * per_cell) + others[1] * per_cell + inner
        )
    for t in range(4):
        for k in range(neigh):
            oh[t * atoms : (t + 1) * atoms, k * atoms : (k + 1) * atoms] = jnp.where(
                ids[t] == nbr_c[k : k + 1], 1.0, 0.0
            ).astype(bf16)
    for load in loads[5:]:
        load.wait()
    elements = embed.shape[0]
    emb[...] = jnp.zeros_like(emb)
    emb[0:elements, :] = embed[...]
    table = emb[...]
    lifted_zero = dot3(table, w_up[0], (1, 0)).T
    el_iota = lax.broadcasted_iota(jnp.int32, (table.shape[0], atoms), 0)
    own_el = jnp.where(el_iota == spe_c, 1.0, 0.0).astype(bf16)
    initial = pick(table.T, own_el)
    first_col = to_col(rfirst[...])
    last_col = to_col(rlast[...])

    for copy in copies:
        copy.wait()

    lane_bits = [(lax.broadcasted_iota(jnp.int32, (8, atoms), 1) // (per_cell * w)) % 2 for w in (4, 2, 1)]
    pieces = [jnp.where(row8 == 3, jnp.broadcast_to(spe_c, (8, atoms)).astype(f32), pos_c)]
    for axis in range(3):
        low = lane_bits[axis] == 1
        where_pos = jnp.where(low, recvp[2 * axis], recvp[2 * axis + 1])
        shifted = where_pos + jnp.where(low, -box_side, box_side)
        where_pos = jnp.where(row8 == axis, shifted, where_pos)
        where_el = jnp.where(low, reccs[2 * axis], reccs[2 * axis + 1]).astype(f32)
        pieces.append(jnp.where(row8 == 3, where_el, where_pos))
    ext = jnp.concatenate(pieces, axis=1)
    ext3 = jnp.concatenate([parts3(ext), jnp.zeros_like(ext)], axis=0).astype(bf16)
    far = dot(ext3, oh[...], (1, 0))
    far = far[0:8] + far[8:16] + far[16:24]
    ev = far - jnp.concatenate([pos_c] * neigh, axis=1)
    far_el = far[3:4].astype(jnp.int32)
    for k in range(neigh):
        cols = slice(k * atoms, (k + 1) * atoms)
        soh[:, cols] = jnp.where(el_iota == far_el[:, cols], 1.0, 0.0).astype(bf16)
    r2 = ev[0:1] * ev[0:1] + ev[1:2] * ev[1:2] + ev[2:3] * ev[2:3]
    radius = jnp.sqrt(r2 + soften)
    inv = 1.0 / radius
    room = jnp.maximum(0.0, 1.0 - radius * radius / (cutoff * cutoff))
    env = room * room
    d_env = room * radius * (-4.0 / (cutoff * cutoff))
    bessels = w_ri.shape[1]
    harm = (lax.broadcasted_iota(jnp.int32, (bessels, edges), 0) + 1).astype(f32)
    sn, cs = sin_cos_pi(harm * (radius * (1.0 / cutoff)))
    amp = math.sqrt(2.0 / cutoff) * inv
    bessel = sn * (amp * env)
    d_bessel = amp * (env * (harm * (math.pi / cutoff) * cs - sn * inv) + sn * d_env)
    dirs[...] = ev * inv

    chunk = 32

    def radial(layer):
        x = dot3_tall(w_ri[layer], bessel)
        pre[layer] = x
        rad[layer] = dot3_tall(w_ro[layer], x * sigmoid(x))

    def forward(layer):
        for c in range(0, chans, chunk):
            s = v0 = v1 = v2 = None
            for k in range(neigh):
                cols = pl.ds(k * atoms, atoms)
                p = picked[layer, pl.ds(c, chunk), cols]
                a = rad[layer, pl.ds(c, chunk), cols] * p
                b = rad[layer, pl.ds(chans + c, chunk), cols] * p
                d = [dirs[pl.ds(m, 1), cols] for m in range(3)]
                if k == 0:
                    s, v0, v1, v2 = a, d[0] * b, d[1] * b, d[2] * b
                else:
                    s, v0, v1, v2 = s + a, v0 + d[0] * b, v1 + d[1] * b, v2 + d[2] * b
            s = s * scaling
            vs = [v * scaling for v in (v0, v1, v2)]
            rows = pl.ds(c, chunk)
            for m in range(3):
                feats[layer, 3 + m, rows, :] = vs[m]
            feats[layer, 0, rows, :] = s
            feats[layer, 1, rows, :] = vs[0] * vs[0] + vs[1] * vs[1] + vs[2] * vs[2]
            feats[layer, 2, rows, :] = s * s
        stacked = feats[layer, 0:3].reshape(3 * chans, atoms)
        return dot3(w_mix[layer].reshape(3 * chans, chans), stacked, (0, 0))

    def backward(layer, d_mix, with_pick):
        d_st = dot3(w_mix[layer].reshape(3 * chans, chans), d_mix, (1, 0))
        d_s = d_st[0:chans] + 2.0 * feats[layer, 0] * d_st[2 * chans :]
        grads[0] = d_s * scaling
        twice = d_st[chans : 2 * chans] * (2.0 * scaling)
        for m in range(3):
            grads[1 + m] = feats[layer, 3 + m] * twice
        for k in range(neigh):
            cols = pl.ds(k * atoms, atoms)
            d = [dirs[pl.ds(m, 1), cols] for m in range(3)]
            acc = [jnp.zeros((8, atoms), f32)] * 3
            for c in range(0, chans, chunk):
                rows = pl.ds(c, chunk)
                g = [grads[m, rows, :] for m in range(4)]
                p = picked[layer, rows, cols]
                b = rad[layer, pl.ds(chans + c, chunk), cols]
                t = d[0] * g[1] + d[1] * g[2] + d[2] * g[3]
                d_rad[rows, cols] = g[0] * p
                d_rad[pl.ds(chans + c, chunk), cols] = t * p
                if with_pick:
                    d_pick[rows, cols] = g[0] * rad[layer, rows, cols] + t * b
                q = b * p
                acc = [
                    acc[m] + jnp.sum((g[1 + m] * q).reshape(chunk // 8, 8, atoms), axis=0)
                    for m in range(3)
                ]
            for m in range(3):
                ddir[layer, pl.ds(m, 1), cols] = jnp.sum(acc[m], axis=0, keepdims=True)

    def backward_radial(layer):
        d_hidden = dot3(w_ro[layer], d_rad[...], (1, 0))
        x = pre[layer]
        sig = sigmoid(x)
        return dot3(w_ri[layer], d_hidden * sig * (1.0 + x * (1.0 - sig)), (1, 0))

    ddir[...] = jnp.zeros_like(ddir)
    radial(0)
    picked[0] = pick(lifted_zero, soh[...])
    layer_out = initial + forward(0)
    lifted = dot3(layer_out, w_up[1], (0, 0))
    grid = (2, 2, 2, per_cell, chans)
    lsend[...] = lifted.reshape(grid)

    def part(ref, axis, side):
        return ref.at[(slice(None),) * axis + (side,)]

    copies = []
    for axis in range(3):
        for side, step in ((1, 1), (0, -1)):
            i = 2 * axis + side
            copies.append(
                remote(part(lsend, axis, side), part(tables.at[axis], axis, side), l_s.at[i], l_r.at[i], face_shift(axis, step))
            )
    for copy in copies:
        copy.start()
    radial(1)
    own_pick = pick(lifted.T, oh[0:atoms, :])
    for copy in copies:
        copy.wait()
    ghosts = jnp.concatenate([tables[a].reshape(atoms, chans).T for a in range(3)], axis=1)
    picked[1] = own_pick + pick(ghosts, oh[atoms:, :])
    second = layer_out + forward(1)
    x2 = dot3(rhid[...], second, (1, 0))
    sig2 = sigmoid(x2)
    energy = jnp.sum(first_col * layer_out, axis=0, keepdims=True) + jnp.sum(
        last_col * (x2 * sig2), axis=0, keepdims=True
    )
    d_second = dot3(rhid[...], last_col * (sig2 * (1.0 + x2 * (1.0 - sig2))), (0, 0))
    backward(1, d_second, True)
    d_both = jnp.concatenate(split2(d_pick[...]), axis=0)
    d_ext = dot(oh[atoms:, :], d_both, (1, 1))
    d_ext = d_ext[:, :chans] + d_ext[:, chans:]
    for axis in range(3):
        back[axis] = d_ext[axis * atoms : (axis + 1) * atoms].reshape(grid)
    copies = []
    for axis in range(3):
        for side, step in ((1, -1), (0, 1)):
            i = 2 * axis + side
            copies.append(
                remote(part(back.at[axis], axis, side), part(backs.at[axis], axis, side), b_s.at[i], b_r.at[i], face_shift(axis, step))
            )
    for copy in copies:
        copy.start()
    d_bes = backward_radial(1)
    d_own = dot(oh[0:atoms, :], d_both, (1, 1))
    d_lifted = d_own[:, :chans] + d_own[:, chans:]
    for copy in copies:
        copy.wait()
    for axis in range(3):
        d_lifted = d_lifted + backs[axis].reshape(atoms, chans)
    d_layer = d_second + first_col + dot3(w_up[1], d_lifted, (1, 1))
    backward(0, d_layer, False)
    d_bes = d_bes + backward_radial(0)
    d_dir = ddir[0] + ddir[1]
    along = d_dir * ev
    d_radius = jnp.sum(d_bes * d_bessel, axis=0, keepdims=True) - (
        along[0:1] + along[1:2] + along[2:3]
    ) * (inv * inv)
    edge_row = lax.broadcasted_iota(jnp.int32, (8, edges), 0)
    eg = jnp.where(edge_row < 3, d_dir * inv + ev * (d_radius * inv), 0.0)

    eg3 = jnp.concatenate([parts3(eg), jnp.zeros_like(eg)], axis=0).astype(bf16)
    spread = dot(eg3, oh[...], (1, 1))
    spread = spread[0:8] + spread[8:16] + spread[16:24]
    for axis in range(3):
        fsend[axis] = spread[:, (axis + 1) * atoms : (axis + 2) * atoms]
    copies = []
    for axis in range(3):
        for face, step in ((2 * axis, -1), (2 * axis + 1, 1)):
            copies.append(remote(fsend.at[axis], frecv.at[face], f_s.at[face], f_r.at[face], face_shift(axis, step)))
    for copy in copies:
        copy.start()
    redstage[...] = jnp.zeros_like(redstage)

    def over_slots(x):
        total = x[:, 0:atoms]
        for k in range(1, neigh):
            total = total + x[:, k * atoms : (k + 1) * atoms]
        return total

    for r in range(3):
        redstage[3 * r : 3 * r + 3, :] = -over_slots(ev[r : r + 1] * eg)[0:3]
    redstage[9:10, :] = energy
    structs = SLAB_STRUCTS * nx
    if one_step:
        slab_row = lax.broadcasted_iota(jnp.int32, (8, atoms), 0) + me["gx"] * SLAB_STRUCTS
        local = jnp.where(slab_row == sid_c, 1.0, 0.0).astype(bf16)
        shares = dot(local, parts3(redstage[...]).astype(bf16), (1, 1))
        shares = shares[:, 0:16] + shares[:, 16:32] + shares[:, 32:48]
        red[...] = shares[0:SLAB_STRUCTS]
        my_slot = (me["gx"] * ny + me["gy"]) * nz + me["gz"]
        first_shifts = all_shifts
    else:
        member = jnp.where(
            lax.broadcasted_iota(jnp.int32, (structs, atoms), 0) == sid_c, 1.0, 0.0
        ).astype(bf16)
        shares = dot(parts3(redstage[...]).astype(bf16), member, (1, 1))
        red[...] = shares[0:16] + shares[16:32] + shares[32:48]
        my_slot = me["gy"] * nz + me["gz"]
        first_shifts = slab_shifts
    sums = []
    for i, shift in enumerate(first_shifts):
        sums.append(remote(red, slab_buf.at[my_slot], a_s.at[i], a_r.at[i], shift))
    for copy in sums:
        copy.start()

    own = spread[:, 0:atoms] - over_slots(eg)
    slab_buf[my_slot] = red[...]
    if not one_step:
        for copy in sums:
            copy.wait()
        total = slab_buf[0]
        for i in range(1, ny * nz):
            total = total + slab_buf[i]
        gx_send[...] = total
        sums = []
        for i, shift in enumerate(gx_shifts):
            sums.append(remote(gx_send, gx_buf.at[i], g_s.at[i], g_r.at[i], shift))
        for copy in sums:
            copy.start()
    for copy in copies:
        copy.wait()
    for axis in range(3):
        own = own + jnp.where(lane_bits[axis] == 1, frecv[2 * axis], frecv[2 * axis + 1])
    order = jnp.where(own_slot == iota1, 1.0, 0.0).astype(bf16)
    own3 = jnp.concatenate([parts3(-own), jnp.zeros_like(own)], axis=0).astype(bf16)
    forces = dot(own3, order, (1, 0))
    packed[16:19, 0:atoms] = (forces[0:8] + forces[8:16] + forces[16:24])[0:3]
    for copy in sums:
        copy.wait()
    if one_step:
        for g in range(nx):
            total = slab_buf[g * ny * nz]
            for i in range(1, ny * nz):
                total = total + slab_buf[g * ny * nz + i]
            gx_send[g * SLAB_STRUCTS : (g + 1) * SLAB_STRUCTS, :] = total
        total = gx_send[...].T
    else:
        for i in range(len(gx_shifts)):
            total = total + gx_buf[i]
    packed[0:16, 0:structs] = total


def in_one_step(counts):
    return math.prod(counts) <= 64


def unpack(packed, en_out, vir_out, f_out):
    structs = en_out.shape[1]
    en_out[...] = packed[9:10, 0:structs]
    vir_out[...] = packed[0:9, 0:structs]
    f_out[...] = packed[16:19, 0 : f_out.shape[1]]


def shards(counts, *args):
    (positions, species, cell_map, neighbours, struct_ids, embed, w_up, w_rad_in, w_rad_out,
     w_mix, read_first, read_hidden, read_last) = args
    nx, ny, nz = counts
    atoms = positions.shape[1]
    neigh = neighbours.shape[0]
    edges = neigh * atoms
    chans = embed.shape[1]
    hidden = w_rad_in.shape[2]
    per_cell = atoms // 8
    structs = SLAB_STRUCTS * nx
    el_rows = -(-embed.shape[0] // 128) * 128
    grid = (2, 2, 2, per_cell, chans)
    operands = (
        positions, species[None], cell_map, neighbours, struct_ids[None], embed, w_up,
        w_rad_in, w_rad_out, w_mix, read_first[None], read_hidden.T, read_last[None],
    )
    one_step = in_one_step(counts)
    share = (SLAB_STRUCTS, 16) if one_step else (16, structs)
    groups = nx * ny * nz if one_step else ny * nz
    dma = pltpu.SemaphoreType.DMA
    vm = lambda *shape: pltpu.VMEM(shape, f32)
    vmem = pl.BlockSpec(memory_space=pltpu.VMEM)
    packed = pl.pallas_call(
        functools.partial(kernel, counts),
        out_shape=jax.ShapeDtypeStruct((24, max(atoms, structs)), f32),
        in_specs=[pl.BlockSpec(memory_space=pltpu.HBM)] * 13,
        out_specs=vmem,
        scratch_shapes=[
            vm(-(-neigh // 8) * 8 + 8, atoms),
            vm(el_rows, chans),
            pltpu.VMEM((4 * atoms, edges), bf16),
            pltpu.VMEM((el_rows, edges), bf16),
            vm(8, edges),
            vm(2, hidden, edges),
            vm(2, 2 * chans, edges),
            vm(2, chans, edges),
            vm(4, chans, atoms),
            vm(2 * chans, edges),
            vm(chans, edges),
            vm(2, 8, edges),
            vm(2, 6, chans, atoms),
            vm(8, atoms),
            pltpu.VMEM((8, atoms), jnp.int32),
            vm(6, 8, atoms),
            pltpu.VMEM((6, 8, atoms), jnp.int32),
            vm(*grid),
            vm(3, *grid),
            vm(3, *grid),
            vm(3, *grid),
            vm(3, 8, atoms),
            vm(6, 8, atoms),
            vm(*share),
            vm(16, atoms),
            vm(groups, *share),
            vm(*((structs, 16) if one_step else share)),
            vm(max(nx - 1, 1), 16, structs),
        ]
        + [pltpu.VMEM(x.shape, x.dtype) for x in operands]
        + [dma((13,))]
        + [dma((6,))] * 10
        + [dma((groups - 1,))] * 2
        + [dma((max(nx - 1, 1),))] * 2,
        compiler_params=pltpu.CompilerParams(
            collective_id=0, has_side_effects=True, vmem_limit_bytes=60 * 1024 * 1024
        ),
    )(*operands)
    energies, virials, forces = pl.pallas_call(
        unpack,
        out_shape=(
            jax.ShapeDtypeStruct((1, structs), f32),
            jax.ShapeDtypeStruct((9, structs), f32),
            jax.ShapeDtypeStruct((3, atoms), f32),
        ),
        in_specs=[vmem],
        out_specs=(vmem, vmem, vmem),
        compiler_params=pltpu.CompilerParams(vmem_limit_bytes=60 * 1024 * 1024),
    )(packed)
    return energies[0], virials, forces


def solution(mesh):
    counts = tuple(mesh.shape[axis] for axis in AXES)
    return jax.shard_map(
        functools.partial(shards, counts),
        mesh=mesh,
        in_specs=(P(None, AXES), P(AXES), P(AXES, None), P(None, AXES), P(AXES))
        + (P(),) * 8,
        out_specs=(P(), P(), P(None, AXES)),
        check_vma=False,
    )
```
